512 devices in a mesh: group: 16 (over x, z_hi), shard: 32 (over y, z_lo, core).
Axes of the slice: x: 4, y: 8, z: 8 (z_hi: 4, z_lo: 2; z = z_hi * 2 + z_lo), core: 2. Of those that a mesh axis runs over, the one named last changes fastest.
Arguments:
- tokens: bfloat16 [32768, 2048], P(('group', 'shard')), may hold values from -7 to 7
- w_qk: bfloat16 [2048, 1024], P('shard'), may hold values from -0.09375 to 0.09375
- w_in: bfloat16 [128, 2048], replicated, may hold values from -0.5 to 0.5
- w_out: bfloat16 [2048, 128], replicated, may hold values from -0.125 to 0.125
- particles: bfloat16 [2097152, 128], P(('group', 'shard')), may hold values from -6 to 6
- cotangent: bfloat16 [2097152, 128], P(('group', 'shard')), may hold values from -6 to 6
- clusters: int32 [2097152], P(('group', 'shard')), may hold values from 0 to 63
- owners: int32 [16384], P(('group', 'shard')), may hold values from 0 to 31, as said below
Outputs:
- particle_out: bfloat16 [2097152, 128], P(('group', 'shard'))
- qk_grad: float32 [2048, 1024], P('shard')
The draws below stay inside these ranges and needn't reach their ends.
Inputs may be any that keep to these rules, and one draw needn't show every extreme that they name: `owners`: each device's blocks name one owner at most 2 times; in every group some owner is named exactly 2 times by the blocks of every device of the group.
All inputs are finite; a program needn't handle non-finite values.
Results may differ from the reference program's by a relative error of at most 0.028.
Values may be sent and summed in bfloat16 or wider, within the bound.
A program may use at most 64 MiB of HBM per device.

```python
import math
import jax
import jax.numpy as jnp
import numpy as np
from jax import lax

D = 2048
HEADS = 8
PW = 128
BLOCK = 128
T_DEV = 64
NB = 32
P_DEV = 4096
PARTICLES = 2097152
TOKENS = 32768
QK = 1024
N_GROUP = 16
N_SHARD = 32


def draw_tokens(key, part):
    key_base = jax.random.fold_in(key, 11)
    return jnp.clip(jax.random.normal(key_base, (TOKENS, D), jnp.float32), -6.0, 6.0).astype(jnp.bfloat16)


def draw_owners(key, part):
    capacity = 2 * NB // N_SHARD
    num_devices = N_GROUP * N_SHARD
    slot_count = N_SHARD * capacity
    key_busy = jax.random.fold_in(key, 21)
    key_noise = jax.random.fold_in(key, 22)
    key_shuffle = jax.random.fold_in(key, 23)
    busiest = jax.random.randint(key_busy, (N_GROUP,), 0, N_SHARD)
    busiest_dev = jnp.repeat(busiest, N_SHARD)
    slot_owner = jnp.arange(slot_count, dtype=jnp.int32) // capacity
    noise_bits = jax.random.randint(key_noise, (num_devices, slot_count), 0, 1 << 20)
    slot_score = jnp.where(slot_owner[None, :] == busiest_dev[:, None], 0, noise_bits + 1)
    slot_score = slot_score * slot_count + jnp.arange(slot_count, dtype=jnp.int32)[None, :]
    slot_order = jnp.argsort(slot_score, axis=1)
    chosen = jnp.take(slot_owner, slot_order[:, :NB])
    shuffle_score = jax.random.randint(key_shuffle, (num_devices, NB), 0, 1 << 20) * NB + jnp.arange(NB, dtype=jnp.int32)[None, :]
    shuffle = jnp.argsort(shuffle_score, axis=1)
    chosen = jnp.take_along_axis(chosen, shuffle, axis=1)
    return chosen.reshape(num_devices * NB).astype(jnp.int32)


def plant(result, stream_key, low, top_value):
    extent = result.shape
    place = [jax.random.randint(jax.random.fold_in(stream_key, axis), (), 0, extent[axis]) for axis in range(len(extent))]
    result = result.at[tuple(place)].set(low)
    longest = extent.index(max(extent))
    place[longest] = (place[longest] + 1) % extent[longest]
    return result.at[tuple(place)].set(top_value)


def block_levels(rng, shape, shards, low, high):
    factor_of, own = 1.0, jax.random.fold_in(rng, 6)
    for dim, blocks in shards:
        heights = jnp.exp(jax.random.uniform(jax.random.fold_in(own, dim), (blocks,), jnp.float32, low / len(shards), high / len(shards)))
        factor_of = factor_of * jnp.repeat(heights, shape[dim] // blocks).reshape([-1 if axis == dim else 1 for axis in range(len(shape))])
    return factor_of


def cumulative_ranks(count, slope):
    loads = [(1 << 20) // math.isqrt(standing ** slope) + 1 for standing in range(1, count + 1)]
    width = 1 + sum(loads) // (1 << 30)
    return np.cumsum(np.array([max(1, weight // width) for weight in loads]))


def ranked_ids(own_key, shape, number_of, skew):
    table = cumulative_ranks(number_of, skew)
    lot = jax.random.randint(jax.random.fold_in(own_key, 1), shape, 0, int(table[number_of - 1]))
    rank = jnp.searchsorted(jnp.asarray(table, jnp.int32), lot, side="right")
    return jax.random.permutation(jax.random.fold_in(own_key, 2), number_of)[rank].astype(jnp.int32)


def scatter_about(key, shape, deviation, bound, split=(), kind=jnp.bfloat16):
    drawn = jax.random.normal(key, shape, jnp.float32) * deviation
    if len(split) > 0:
        drawn = block_levels(key, shape, split, -0.22, 0.18) * drawn
    return jnp.clip(drawn, min=-bound, max=bound).astype(kind)


def setup_inputs(seed: int = 0) -> dict:
    key_list = jax.random.split(jax.random.key(seed), 9)
    return {
        "tokens": draw_tokens(jax.random.fold_in(key_list[8], 71), 0),
        "w_qk": scatter_about(key_list[1], (D, QK), (2 * D) ** -0.5, 0.09375, ((0, 32),)),
        "w_in": scatter_about(key_list[2], (PW, D), PW ** -0.5, 0.5),
        "w_out": scatter_about(key_list[3], (D, PW), D ** -0.5, 0.125),
        "particles": scatter_about(key_list[4], (PARTICLES, PW), 1.0, 6.0, ((0, 512),)),
        "cotangent": scatter_about(key_list[5], (PARTICLES, PW), 1.0, 6.0, ((0, 512),)),
        "clusters": plant(ranked_ids(key_list[6], (PARTICLES,), T_DEV, 2), jax.random.fold_in(key_list[6], 3), 0, T_DEV - 1).astype(jnp.int32),
        "owners": draw_owners(jax.random.fold_in(key_list[8], 71), 0),
    }


def token_pass(tokens, pooled, w_qk, w_in, w_out, pooled_grad):
    hidden_sum = tokens.astype(jnp.float32) + jnp.dot(pooled, w_in, preferred_element_type=jnp.float32)
    hidden = hidden_sum.astype(jnp.bfloat16)
    queries = jnp.dot(hidden, w_qk, preferred_element_type=jnp.float32).astype(jnp.bfloat16)
    num_rows = hidden.shape[0]
    head_cols = queries.shape[1]
    q_heads = queries.reshape(num_rows, HEADS, -1).astype(jnp.float32)
    score_scale = 1.0 / math.sqrt(q_heads.shape[2])
    scores = jnp.einsum('ihd,jhd->hij', q_heads, q_heads) * score_scale
    self_mask = jnp.eye(num_rows, dtype=bool)
    scores = jnp.where(self_mask[None], -1000000000.0, scores)
    row_max = lax.optimization_barrier(jnp.max(scores, axis=2, keepdims=True))
    weights_exp = jnp.exp(scores - row_max)
    attn_prob = weights_exp / lax.optimization_barrier(jnp.sum(weights_exp, axis=2, keepdims=True))
    prob_low = lax.optimization_barrier(attn_prob.astype(jnp.bfloat16)).astype(jnp.float32)
    hidden_wide = hidden.astype(jnp.float32)
    values = hidden_wide[:, :head_cols].reshape(num_rows, HEADS, -1)
    attended = jnp.einsum('hij,jhv->ihv', prob_low, values).reshape(num_rows, head_cols)
    output = jnp.concatenate([hidden_wide[:, :head_cols] + attended, hidden_wide[:, head_cols:]], axis=1).astype(jnp.bfloat16)
    unpooled = jnp.dot(output, w_out, preferred_element_type=jnp.float32).astype(jnp.bfloat16)
    out_grad = jnp.dot(pooled_grad, w_out.T, preferred_element_type=jnp.float32).astype(jnp.bfloat16)
    grad_heads = out_grad[:, :head_cols].reshape(num_rows, HEADS, -1).astype(jnp.float32)
    prob_grad = jnp.einsum('ihv,jhv->hij', grad_heads, values)
    score_grad = attn_prob * (prob_grad - lax.optimization_barrier(jnp.sum(prob_grad * attn_prob, axis=2, keepdims=True))) * score_scale
    score_low = lax.optimization_barrier(score_grad.astype(jnp.bfloat16)).astype(jnp.float32)
    q_grad = jnp.einsum('hij,jhd->ihd', score_low, q_heads) + jnp.einsum('hji,jhd->ihd', score_low, q_heads)
    q_grad = q_grad.reshape(num_rows, -1).astype(jnp.bfloat16)
    return (unpooled, hidden, q_grad)

def reference(tokens, w_qk, w_in, w_out, particles, cotangent, clusters, owners):
    block_owner = jnp.repeat(owners, BLOCK)
    device_ids = jnp.arange(PARTICLES, dtype=jnp.int32) // P_DEV
    group_ids = device_ids // N_SHARD
    token_ids = ((group_ids * N_SHARD + block_owner) * T_DEV + clusters).astype(jnp.int32)
    counts = jax.ops.segment_sum(jnp.ones((PARTICLES,), jnp.float32), token_ids, TOKENS)
    pooled_sum = jax.ops.segment_sum(particles.astype(jnp.float32), token_ids, TOKENS)
    pooled = (pooled_sum / jnp.maximum(counts, 1.0)[:, None]).astype(jnp.bfloat16)
    pooled_grad = jax.ops.segment_sum(cotangent.astype(jnp.float32), token_ids, TOKENS).astype(jnp.bfloat16)
    num_devices = N_GROUP * N_SHARD

    def device_step(carry, inputs):
        tok_rows, pool_rows, grad_rows = inputs
        unpooled, hidden, q_grad = token_pass(tok_rows, pool_rows, w_qk, w_in, w_out, grad_rows)
        term = jnp.dot(hidden.T, q_grad, preferred_element_type=jnp.float32)
        term = lax.optimization_barrier(term.astype(jnp.bfloat16)).astype(jnp.float32)
        return (carry + term, unpooled)
    start_sum = jnp.zeros((D, QK), jnp.float32)
    qk_grad, unpooled = lax.scan(device_step, start_sum, (tokens.reshape(num_devices, T_DEV, D), pooled.reshape(num_devices, T_DEV, PW), pooled_grad.reshape(num_devices, T_DEV, PW)))
    all_unpooled = unpooled.reshape(TOKENS, PW)
    gathered = jnp.take(all_unpooled, token_ids, axis=0).astype(jnp.float32)
    particle_out = (particles.astype(jnp.float32) + gathered).astype(jnp.bfloat16)
    return (particle_out, qk_grad)
```

```python
import functools
import math

import jax
import jax.numpy as jnp
from jax import lax
from jax.experimental import pallas as pl
from jax.experimental.pallas import tpu as pltpu
from jax.sharding import PartitionSpec as P

NX = 4
HEAD = 128
TOK = 64
BLOCK = 128
MESH = pl.DeviceIdType.MESH
F32 = jnp.float32
BF16 = jnp.bfloat16


def dot(a, b, dims=((1,), (0,))):
    return lax.dot_general(a, b, (dims, ((), ())), preferred_element_type=F32)


def iota(shape, dim):
    return lax.broadcasted_iota(jnp.int32, shape, dim)


def pool_kernel(n_owner, per_step, owners, clusters, feat, grad, part, cnt, acc):
    step = pl.program_id(0)

    @pl.when(step == 0)
    def _():
        acc[...] = jnp.zeros_like(acc)
        cnt[...] = jnp.zeros_like(cnt)

    ones = jnp.ones((8, BLOCK), BF16)
    for i in range(per_step):
        owner = owners[step * per_step + i]
        slot = (owner % 2) * (n_owner // 2) + ((owner // 2) % 2) * (n_owner // 4) + owner // 4
        labels = clusters[pl.ds(i, 1), :]
        member = (iota((BLOCK, BLOCK), 0) == labels).astype(F32).astype(BF16)
        rows = pl.ds(i * BLOCK, BLOCK)
        both = jnp.concatenate([feat[rows, :], grad[rows, :]], axis=1)
        acc[slot] += dot(member[:TOK], both)
        cnt[owner // 4, pl.ds(owner % 4, 1), :] += dot(ones, member, ((1,), (1,)))[:1]

    @pl.when(step == pl.num_programs(0) - 1)
    def _():
        for k in range(n_owner):
            part[k] = acc[k].astype(BF16)


def pool(owners, clusters, feat, grad, n_owner):
    nb = owners.shape[0]
    per_step = 8
    return pl.pallas_call(
        functools.partial(pool_kernel, n_owner, per_step),
        out_shape=(
            jax.ShapeDtypeStruct((n_owner, TOK, 2 * BLOCK), BF16),
            jax.ShapeDtypeStruct((n_owner // 4, 8, BLOCK), F32),
        ),
        grid=(nb // per_step,),
        in_specs=[
            pl.BlockSpec(memory_space=pltpu.SMEM),
            pl.BlockSpec((per_step, BLOCK), lambda i: (i, 0)),
            pl.BlockSpec((per_step * BLOCK, BLOCK), lambda i: (i, 0)),
            pl.BlockSpec((per_step * BLOCK, BLOCK), lambda i: (i, 0)),
        ],
        out_specs=(
            pl.BlockSpec((n_owner, TOK, 2 * BLOCK), lambda i: (0, 0, 0)),
            pl.BlockSpec((n_owner // 4, 8, BLOCK), lambda i: (0, 0, 0)),
        ),
        scratch_shapes=[pltpu.VMEM((n_owner, TOK, 2 * BLOCK), F32)],
    )(owners, clusters, feat, grad)


def unpool_kernel(per_step, owners, clusters, feat, table, out):
    step = pl.program_id(0)
    for i in range(per_step):
        owner = owners[step * per_step + i]
        labels = clusters[pl.ds(i, 1), :]
        member = (iota((TOK, BLOCK), 0) == labels).astype(F32).astype(BF16)
        rows = pl.ds(i * BLOCK, BLOCK)
        picked = dot(member, table[owner], ((0,), (0,)))
        out[rows, :] = (feat[rows, :].astype(F32) + picked).astype(BF16)


def unpool(owners, clusters, feat, table):
    nb = owners.shape[0]
    per_step = 8
    return pl.pallas_call(
        functools.partial(unpool_kernel, per_step),
        out_shape=jax.ShapeDtypeStruct(feat.shape, BF16),
        grid=(nb // per_step,),
        in_specs=[
            pl.BlockSpec(memory_space=pltpu.SMEM),
            pl.BlockSpec((per_step, BLOCK), lambda i: (i, 0)),
            pl.BlockSpec((per_step * BLOCK, BLOCK), lambda i: (i, 0)),
            pl.BlockSpec(table.shape, lambda i: (0, 0, 0)),
        ],
        out_specs=pl.BlockSpec((per_step * BLOCK, BLOCK), lambda i: (i, 0)),
    )(owners, clusters, feat, table)


def layer_kernel(
    nx, nzh, ny, n_sem,
    part, cnt, w, tok, w_in, w_out,
    table_out, fin_out,
    pc, ps1, pz, ps2, py, cy, c1, cr, c2, cq, wb, tk, pl4, hid, up, ur, ub,
    ga, gb, gca, gcb, gsa, gsb, gya, gzb, ra, rb, qa, qb, fz, fx,
    send, recv,
):
    g = lax.axis_index("group")
    s = lax.axis_index("shard")
    x = g // nzh
    zh = g % nzh
    y = s // 4
    z = (s // 2) % 2
    c = s % 2
    zc = s % 4
    nz = 2 * nzh
    zz = zh * 2 + z
    d = hid.shape[1]
    cols = 2 * HEAD
    quarter = TOK // nzh

    core = (g, s + 1 - 2 * c)
    zpair = (g, s + 2 - 4 * z)

    def ydev(o):
        return (g, ((y + o) % ny) * 4 + zc)

    def xdev(o):
        return (((x + o) % nx) * nzh + zh, s)

    def zdev(o):
        t = (zz + o) % nz
        return (x * nzh + t // 2, y * 4 + (t % 2) * 2 + c)

    def zhdev(o):
        return (x * nzh + (zh + o) % nzh, s)

    used = []

    def copy(src, dst, dev):
        i = len(used)
        assert i < n_sem
        r = pltpu.make_async_remote_copy(
            src_ref=src, dst_ref=dst, send_sem=send.at[i], recv_sem=recv.at[i],
            device_id=dev, device_id_type=MESH,
        )
        used.append(r)
        r.start()
        return r

    peers = [core] + [ydev(o) for o in range(1, ny)] + [xdev(o) for o in range(1, nx)]
    peers += [zdev(o) for o in range(1, nz)]
    barrier = pltpu.get_barrier_semaphore()
    for dev in peers:
        pl.semaphore_signal(barrier, inc=1, device_id=dev, device_id_type=MESH)
    pl.semaphore_wait(barrier, len(peers))

    first = copy(part.at[1 - c, 1 - z], pc.at[1 - z], core)
    second = copy(part.at[1 - c, z], pc.at[z], core)
    counts_y = [copy(cnt.at[(y + o) % ny], cy.at[y], ydev(o)) for o in range(1, ny)]
    mine = pl.ds(pl.multiple_of(x * cols, cols), cols)
    w_y = [copy(w.at[:, mine], wb.at[y, zc], ydev(o)) for o in range(1, ny)]
    tok_x = [copy(tok, tk.at[x], xdev(o)) for o in range(1, nx)]
    wb[y, zc] = w[:, mine]
    tk[x] = tok[...]

    first.wait_recv()
    for k in range(ny):
        ps1[k] = (part[c, 1 - z, k].astype(F32) + pc[1 - z, k].astype(F32)).astype(BF16)
    pool_z = copy(ps1, pz, zpair)

    total = cnt[y]
    for o, r in enumerate(counts_y):
        r.wait_recv()
        total = total + cy[(y + ny - o - 1) % ny]
    c1[...] = total
    counts_c = copy(c1, cr, core)

    for r in w_y:
        r.wait_recv()
    w_z = copy(wb.at[:, zc], wb.at[:, zc], zpair)
    w_c1 = copy(wb.at[:, zc], wb.at[:, zc], core)

    counts_c.wait_recv()
    c2[...] = c1[...] + cr[...]
    counts_z = copy(c2, cq, zpair)

    second.wait_recv()
    pool_z.wait_recv()
    for k in range(ny):
        ps2[k] = (
            part[c, z, k].astype(F32) + pc[z, k].astype(F32) + pz[k].astype(F32)
        ).astype(BF16)
    pool_y = [copy(ps2.at[(y + o) % ny], py.at[y], ydev(o)) for o in range(1, ny)]

    w_z.wait_recv()
    zc_far = (1 - z) * 2 + c
    w_c2 = copy(wb.at[:, zc_far], wb.at[:, zc_far], core)

    counts_z.wait_recv()
    count = c2[...] + cq[...]
    row = jnp.sum(jnp.where(iota(count.shape, 0) == zc, count, 0.0), axis=0, keepdims=True)
    eye = iota((TOK, HEAD), 0) == iota((TOK, HEAD), 1)
    column = jnp.sum(jnp.where(eye, jnp.broadcast_to(row, (TOK, HEAD)), 0.0), axis=1, keepdims=True)

    sums = ps2[y].astype(F32)
    for o, r in enumerate(pool_y):
        r.wait_recv()
        sums = sums + py[(y + ny - o - 1) % ny].astype(F32)
    pl4[x, :, 0:HEAD] = (sums[:, :HEAD] / jnp.maximum(column, 1.0)).astype(BF16)
    pl4[x, :, HEAD : 2 * HEAD] = sums[:, HEAD:].astype(BF16)
    pool_x = [copy(pl4.at[x], pl4.at[x], xdev(o)) for o in range(1, nx)]

    for r in tok_x:
        r.wait_recv()
    w_c1.wait_recv()
    w_c2.wait_recv()
    for r in pool_x:
        r.wait_recv()

    rows = nx * TOK
    pooled = pl4[:, :, 0:HEAD].reshape(rows, HEAD)
    pooled_grad = pl4[:, :, HEAD : 2 * HEAD].reshape(rows, HEAD)
    step = 512
    for n in range(0, d, step):
        span = slice(n, n + step)
        wide = tk[:, :, span].reshape(rows, step).astype(F32) + dot(pooled, w_in[:, span])
        hid[:, span] = wide.astype(BF16)
    queries = dot(hid[...], wb[...].reshape(d, cols)).astype(BF16)
    head_rows = pl.ds(pl.multiple_of(x * cols, cols), cols)
    tail_rows = pl.ds(pl.multiple_of(nx * cols + x * cols, cols), cols)
    out_grad = dot(pooled_grad, w_out[head_rows, :], ((1,), (1,))).astype(BF16)
    values = hid[:, head_rows]
    scale = 1.0 / math.sqrt(HEAD)
    pair = 2 * TOK
    ii, jj = iota((pair, pair), 0), iota((pair, pair), 1)
    same = (ii // TOK) == (jj // TOK)
    diag = ii == jj
    out_parts, q_parts = [], []
    for p in range(rows // pair):
        ps = slice(p * pair, (p + 1) * pair)
        out_row, q_row = [], []
        for h in range(2):
            hs = slice(h * HEAD, (h + 1) * HEAD)
            q, v, og = queries[ps, hs], values[ps, hs], out_grad[ps, hs]
            scores = dot(q, q, ((1,), (1,))) * scale
            scores = jnp.where(diag, -1000000000.0, scores)
            scores = jnp.where(same, scores, -jnp.inf)
            e = jnp.exp(scores - jnp.max(scores, axis=1, keepdims=True))
            prob = e / jnp.sum(e, axis=1, keepdims=True)
            attended = dot(prob.astype(BF16), v)
            out_row.append((v.astype(F32) + attended).astype(BF16))
            prob_grad = dot(og, v, ((1,), (1,)))
            inner = jnp.sum(prob_grad * prob, axis=1, keepdims=True)
            score_grad = (prob * (prob_grad - inner) * scale).astype(BF16)
            q_row.append((dot(score_grad, q) + dot(score_grad, q, ((0,), (0,)))).astype(BF16))
        out_parts.append(jnp.concatenate(out_row, axis=1))
        q_parts.append(jnp.concatenate(q_row, axis=1))
    out_cols = jnp.concatenate(out_parts, axis=0)
    q_grad = jnp.concatenate(q_parts, axis=0)
    unp = dot(out_cols, w_out[head_rows, :]) + dot(hid[:, tail_rows], w_out[tail_rows, :])
    unp = unp.astype(BF16)
    for k in range(nx):
        up[k] = unp[k * TOK : (k + 1) * TOK]
    unp_x = [copy(up.at[(x + o) % nx], ur.at[x], xdev(o)) for o in range(1, nx)]

    for k in range(2 * ny):
        yk, zk = k // 2, k % 2
        term = dot(hid[:, 2 * TOK * k : 2 * TOK * (k + 1)], q_grad, ((0,), (0,))).astype(BF16)
        for ck in range(2):
            ga[ck, yk, zk] = term[TOK * ck : TOK * (ck + 1), :HEAD]
            for q in range(nzh):
                at = TOK * ck + quarter * q
                gb[ck, zk, q, yk] = term[at : at + quarter, HEAD:]
    grad_a = copy(ga.at[1 - c], gca, core)
    grad_b = copy(gb.at[1 - c], gcb, core)

    sums = up[x].astype(F32)
    for o, r in enumerate(unp_x):
        r.wait_recv()
        sums = sums + ur[(x + nx - o - 1) % nx].astype(F32)
    ub[y, zc] = sums.astype(BF16)
    unp_y = [copy(ub.at[y, zc], ub.at[y, zc], ydev(o)) for o in range(1, ny)]

    grad_a.wait_recv()
    for k in range(ny):
        gsa[k] = (ga[c, k].astype(F32) + gca[k].astype(F32)).astype(BF16)
    ga_y = [copy(gsa.at[(y + o) % ny], gya.at[y], ydev(o)) for o in range(1, ny)]
    grad_b.wait_recv()
    for zk in range(2):
        for q in range(nzh):
            gsb[zk, q] = (gb[c, zk, q].astype(F32) + gcb[zk, q].astype(F32)).astype(BF16)

    def zslot(o):
        t = (zz + o) % nz
        return t % 2, t // 2

    gb_z = [copy(gsb.at[zslot(o)], gzb.at[zz], zdev(o)) for o in range(1, nz)]

    for r in unp_y:
        r.wait_recv()
    unp_z = copy(ub.at[:, zc], ub.at[:, zc], zpair)
    unp_c1 = copy(ub.at[:, zc], ub.at[:, zc], core)

    sums = gsa[y].astype(F32)
    for o, r in enumerate(ga_y):
        r.wait_recv()
        sums = sums + gya[(y + ny - o - 1) % ny].astype(F32)
    for zk in range(2):
        for q in range(nzh):
            ra[zk, q] = sums[zk, quarter * q : quarter * (q + 1)].astype(BF16)
    qa_z = [copy(ra.at[zslot(o)], qa.at[zz], zdev(o)) for o in range(1, nz)]
    sums = gsb[z, zh].astype(F32)
    for o, r in enumerate(gb_z):
        r.wait_recv()
        sums = sums + gzb[(zz + nz - o - 1) % nz].astype(F32)
    rb[...] = sums.astype(BF16)
    qb_y = [copy(rb.at[(y + o) % ny], qb.at[y], ydev(o)) for o in range(1, ny)]

    unp_z.wait_recv()
    unp_c2 = copy(ub.at[:, zc_far], ub.at[:, zc_far], core)

    sums = ra[z, zh].astype(F32)
    for o, r in enumerate(qa_z):
        r.wait_recv()
        sums = sums + qa[(zz + nz - o - 1) % nz].astype(F32)
    fz[zh, :, 0:HEAD] = sums.astype(BF16)
    sums = rb[y].astype(F32)
    for o, r in enumerate(qb_y):
        r.wait_recv()
        sums = sums + qb[(y + ny - o - 1) % ny].astype(F32)
    fz[zh, :, HEAD : 2 * HEAD] = sums.astype(BF16)
    fin_z = [copy(fz.at[zh], fz.at[zh], zhdev(o)) for o in range(1, nzh)]

    unp_c1.wait_recv()
    unp_c2.wait_recv()
    table_out[...] = ub[...].reshape(table_out.shape)

    for r in fin_z:
        r.wait_recv()
    fin_x = [copy(fz, fx.at[x], xdev(o)) for o in range(1, nx)]
    fx[x] = fz[...]
    for r in fin_x:
        r.wait_recv()
    for k in range(nx):
        fin_out[:, cols * k : cols * (k + 1)] = fx[k].reshape(TOK, cols).astype(F32)
    for r in used:
        r.wait_send()


def layer(part, cnt, w, tok, w_in, w_out, nzh, ny):
    nx, nz = NX, 2 * nzh
    d = w_in.shape[1]
    cols = 2 * HEAD
    quarter = TOK // nzh
    n_sem = 2 + 7 * (ny - 1) + 4 * (nx - 1) + 2 * (nz - 1) + (nzh - 1) + 13
    v = lambda *shape: pltpu.VMEM(shape, BF16)
    vf = lambda *shape: pltpu.VMEM(shape, F32)
    scratch = [
        v(2, ny, TOK, cols), v(ny, TOK, cols), v(ny, TOK, cols), v(ny, TOK, cols), v(ny, TOK, cols),
        vf(ny, 8, HEAD), vf(8, HEAD), vf(8, HEAD), vf(8, HEAD), vf(8, HEAD),
        v(ny, 4, TOK, cols), v(nx, TOK, d), v(nx, TOK, cols), v(nx * TOK, d),
        v(nx, TOK, HEAD), v(nx, TOK, HEAD), v(ny, 4, TOK, HEAD),
        v(2, ny, 2, TOK, HEAD), v(2, 2, nzh, ny, quarter, HEAD),
        v(ny, 2, TOK, HEAD), v(2, nzh, ny, quarter, HEAD),
        v(ny, 2, TOK, HEAD), v(2, nzh, ny, quarter, HEAD),
        v(ny, 2, TOK, HEAD), v(nz, ny, quarter, HEAD),
        v(2, nzh, quarter, HEAD), v(ny, quarter, HEAD), v(nz, quarter, HEAD), v(ny, quarter, HEAD),
        v(nzh, quarter, cols), v(nx, nzh, quarter, cols),
        pltpu.SemaphoreType.DMA((n_sem,)), pltpu.SemaphoreType.DMA((n_sem,)),
    ]
    vmem = pl.BlockSpec(memory_space=pltpu.VMEM)
    return pl.pallas_call(
        functools.partial(layer_kernel, nx, nzh, ny, n_sem),
        out_shape=(
            jax.ShapeDtypeStruct((4 * ny, TOK, HEAD), BF16),
            jax.ShapeDtypeStruct((TOK, nx * cols), F32),
        ),
        in_specs=[vmem] * 6,
        out_specs=(vmem, vmem),
        scratch_shapes=scratch,
        compiler_params=pltpu.CompilerParams(collective_id=0, has_side_effects=True),
    )(part, cnt, w, tok, w_in, w_out)


def local(tokens, w_qk, w_in, w_out, particles, cotangent, clusters, owners):
    n_shard = lax.axis_size("shard")
    nzh = lax.axis_size("group") // NX
    ny = n_shard // 4
    labels = clusters.reshape(-1, BLOCK)
    part, cnt = pool(owners, labels, particles, cotangent, n_shard)
    part = part.reshape(2, 2, ny, TOK, 2 * HEAD)
    table, qk_grad = layer(part, cnt, w_qk, tokens, w_in, w_out, nzh, ny)
    particle_out = unpool(owners, labels, particles, table)
    return (particle_out, qk_grad)


def solution(mesh):
    placed = (
        P(("group", "shard"), None),
        P("shard", None),
        P(),
        P(),
        P(("group", "shard"), None),
        P(("group", "shard"), None),
        P(("group", "shard")),
        P(("group", "shard")),
    )
    return jax.shard_map(
        local,
        mesh=mesh,
        in_specs=placed,
        out_specs=(P(("group", "shard"), None), P("shard", None)),
        check_vma=False,
    )
```

```python
import functools
import math

import jax
import jax.numpy as jnp
from jax import lax
from jax.experimental import pallas as pl
from jax.experimental.pallas import tpu as pltpu
from jax.sharding import PartitionSpec as P

NX = 4
HEAD = 128
TOK = 64
BLOCK = 128
MESH = pl.DeviceIdType.MESH
F32 = jnp.float32
BF16 = jnp.bfloat16


def dot(a, b, dims=((1,), (0,))):
    return lax.dot_general(a, b, (dims, ((), ())), preferred_element_type=F32)


def iota(shape, dim):
    return lax.broadcasted_iota(jnp.int32, shape, dim)


def layer_kernel(
    nx, nzh, ny, n_sem,
    owners, first, last, clusters, w, tok, w_in_hbm, w_out_hbm, feat_hbm, cot_hbm,
    p_out, fin_out,
    fv, cv, w_in, w_out, ob, cnt,
    pf, pg, pcf, pcg, fown, gown, fzs, fzr, gzs, gzr, fys, fyr, gys, gyr,
    cy, c1, cr, c2, cq, wb, tk, plf, plg, hid, up, ur, ub,
    ga, gb, gca, gcb, gsa, gsb, gya, gzb, ra, rb, qa, qb, fx,
    send, recv, here,
):
    g = lax.axis_index("group")
    s = lax.axis_index("shard")
    x = g // nzh
    zh = g % nzh
    y = s // 4
    z = (s // 2) % 2
    c = s % 2
    zc = s % 4
    zc_far = (1 - z) * 2 + c
    nz = 2 * nzh
    zz = zh * 2 + z
    d = hid.shape[1]
    cols = 2 * HEAD
    quarter = TOK // nzh
    nb = owners.shape[0]

    core = (g, s + 1 - 2 * c)
    zpair = (g, s + 2 - 4 * z)

    def ydev(o):
        return (g, ((y + o) % ny) * 4 + zc)

    def xdev(o):
        return (((x + o) % nx) * nzh + zh, s)

    def zslot(o):
        t = (zz + o) % nz
        return t % 2, t // 2

    def zdev(o):
        zo, zho = zslot(o)
        return (x * nzh + zho, y * 4 + zo * 2 + c)

    def xzdev(ox, oz):
        return (((x + ox) % nx) * nzh + (zh + oz) % nzh, s)

    xz = [(ox, oz) for ox in range(nx) for oz in range(nzh) if ox or oz]
    used = []

    def copy(src, dst, dev):
        i = len(used)
        assert i < n_sem
        r = pltpu.make_async_remote_copy(
            src_ref=src, dst_ref=dst, send_sem=send.at[i], recv_sem=recv.at[i],
            device_id=dev, device_id_type=MESH,
        )
        used.append(r)
        r.start()
        return r

    peers = [core] + [ydev(o) for o in range(1, ny)] + [zdev(o) for o in range(1, nz)]
    peers += [xzdev(ox, oz) for ox, oz in xz if ox]
    barrier = pltpu.get_barrier_semaphore()
    for dev in peers:
        pl.semaphore_signal(barrier, inc=1, device_id=dev, device_id_type=MESH)
    mine = pl.ds(pl.multiple_of(x * cols, cols), cols)
    loads = [
        pltpu.make_async_copy(feat_hbm, fv, here.at[0]),
        pltpu.make_async_copy(cot_hbm, cv, here.at[1]),
        pltpu.make_async_copy(w.at[:, mine], wb.at[y, zc], here.at[2]),
        pltpu.make_async_copy(tok, tk.at[x], here.at[3]),
        pltpu.make_async_copy(w_in_hbm, w_in, here.at[4]),
        pltpu.make_async_copy(w_out_hbm, w_out, here.at[5]),
    ]
    for r in loads:
        r.start()
    cnt[...] = jnp.zeros_like(cnt)
    pl.semaphore_wait(barrier, len(peers))

    w_y = [copy(w.at[:, mine], wb.at[y, zc], ydev(o)) for o in range(1, ny)]
    tok_x = [copy(tok, tk.at[x], xdev(o)) for o in range(1, nx)]

    ones = jnp.ones((8, 2 * BLOCK), BF16)

    def pooled_sum(yk, zk, ck):
        owner = yk * 4 + zk * 2 + ck
        member, feats, cots = [], [], []
        b0, b1 = first[owner], last[owner]
        for at, valid in ((jnp.minimum(b0, nb - 1), b0 < nb), (jnp.maximum(b1, 0), b1 > b0)):
            labels = jnp.where(valid, clusters[pl.ds(at, 1), :], -1)
            member.append((iota((TOK, BLOCK), 0) == labels).astype(F32).astype(BF16))
            feats.append(fv[at])
            cots.append(cv[at])
        member = jnp.concatenate(member, axis=1)
        both = jnp.concatenate(
            [jnp.concatenate(feats, axis=0), jnp.concatenate(cots, axis=0)], axis=1
        )
        cnt[yk, pl.ds(zk * 2 + ck, 1), 0:TOK] = dot(ones, member, ((1,), (1,)))[:1]
        return dot(member, both)

    loads[0].wait()
    loads[1].wait()
    for yk in range(ny):
        for zk in range(2):
            v = pooled_sum(yk, zk, 1 - c)
            pf[zk, yk] = v[:, :HEAD].astype(BF16)
            pg[zk, yk] = v[:, HEAD:].astype(BF16)
    pool_f = copy(pf, pcf, core)
    pool_g = copy(pg, pcg, core)
    for yk in range(ny):
        for zk in range(2):
            v = pooled_sum(yk, zk, c)
            fown[zk, yk] = v[:, :HEAD]
            gown[zk, yk] = v[:, HEAD:]
    counts_y = [copy(cnt.at[(y + o) % ny], cy.at[y], ydev(o)) for o in range(1, ny)]

    pool_f.wait_recv()
    for k in range(ny):
        fzs[k] = (fown[1 - z, k] + pcf[1 - z, k].astype(F32)).astype(BF16)
    feat_z = copy(fzs, fzr, zpair)
    pool_g.wait_recv()
    for k in range(ny):
        gzs[k] = (gown[1 - z, k] + pcg[1 - z, k].astype(F32)).astype(BF16)
    cot_z = copy(gzs, gzr, zpair)

    feat_z.wait_recv()
    for k in range(ny):
        fys[k] = (fown[z, k] + pcf[z, k].astype(F32) + fzr[k].astype(F32)).astype(BF16)
    feat_y = [copy(fys.at[(y + o) % ny], fyr.at[y], ydev(o)) for o in range(1, ny)]

    total = cnt[y]
    for o, r in enumerate(counts_y):
        r.wait_recv()
        total = total + cy[(y + ny - o - 1) % ny]
    c1[...] = total
    counts_c = copy(c1, cr, core)

    for r in w_y:
        r.wait_recv()
    loads[2].wait()
    w_z = copy(wb.at[:, zc], wb.at[:, zc], zpair)
    w_c1 = copy(wb.at[:, zc], wb.at[:, zc], core)

    counts_c.wait_recv()
    c2[...] = c1[...] + cr[...]
    counts_z = copy(c2, cq, zpair)

    cot_z.wait_recv()
    for k in range(ny):
        gys[k] = (gown[z, k] + pcg[z, k].astype(F32) + gzr[k].astype(F32)).astype(BF16)
    cot_y = [copy(gys.at[(y + o) % ny], gyr.at[y], ydev(o)) for o in range(1, ny)]

    counts_z.wait_recv()
    count = c2[...] + cq[...]
    row = jnp.sum(jnp.where(iota(count.shape, 0) == zc, count, 0.0), axis=0, keepdims=True)
    eye = iota((TOK, HEAD), 0) == iota((TOK, HEAD), 1)
    column = jnp.sum(jnp.where(eye, jnp.broadcast_to(row, (TOK, HEAD)), 0.0), axis=1, keepdims=True)

    sums = fys[y].astype(F32)
    for o, r in enumerate(feat_y):
        r.wait_recv()
        sums = sums + fyr[(y + ny - o - 1) % ny].astype(F32)
    plf[x] = (sums / jnp.maximum(column, 1.0)).astype(BF16)
    feat_x = [copy(plf.at[x], plf.at[x], xdev(o)) for o in range(1, nx)]

    sums = gys[y].astype(F32)
    for o, r in enumerate(cot_y):
        r.wait_recv()
        sums = sums + gyr[(y + ny - o - 1) % ny].astype(F32)
    plg[x] = sums.astype(BF16)
    cot_x = [copy(plg.at[x], plg.at[x], xdev(o)) for o in range(1, nx)]

    for r in loads[3:]:
        r.wait()
    for r in tok_x:
        r.wait_recv()
    for r in feat_x:
        r.wait_recv()

    rows = nx * TOK
    pooled = plf[...].reshape(rows, HEAD)
    step = 512
    for n in range(0, d, step):
        span = slice(n, n + step)
        wide = tk[:, :, span].reshape(rows, step).astype(F32) + dot(pooled, w_in[:, span])
        hid[:, span] = wide.astype(BF16)
    w_z.wait_recv()
    w_c2 = copy(wb.at[:, zc_far], wb.at[:, zc_far], core)
    w_c1.wait_recv()
    w_c2.wait_recv()
    queries = dot(hid[...], wb[...].reshape(d, cols)).astype(BF16)
    head_rows = pl.ds(pl.multiple_of(x * cols, cols), cols)
    tail_rows = pl.ds(pl.multiple_of(nx * cols + x * cols, cols), cols)
    values = hid[:, head_rows]
    scale = 1.0 / math.sqrt(HEAD)
    pair = 2 * TOK
    ii, jj = iota((pair, pair), 0), iota((pair, pair), 1)
    same = (ii // TOK) == (jj // TOK)
    diag = ii == jj
    probs, out_parts = {}, []
    for p in range(rows // pair):
        ps = slice(p * pair, (p + 1) * pair)
        out_row = []
        for h in range(2):
            hs = slice(h * HEAD, (h + 1) * HEAD)
            q, v = queries[ps, hs], values[ps, hs]
            scores = dot(q, q, ((1,), (1,))) * scale
            scores = jnp.where(diag, -1000000000.0, scores)
            scores = jnp.where(same, scores, -jnp.inf)
            e = jnp.exp(scores - jnp.max(scores, axis=1, keepdims=True))
            prob = e / jnp.sum(e, axis=1, keepdims=True)
            probs[p, h] = prob
            attended = dot(prob.astype(BF16), v)
            out_row.append((v.astype(F32) + attended).astype(BF16))
        out_parts.append(jnp.concatenate(out_row, axis=1))
    out_cols = jnp.concatenate(out_parts, axis=0)
    unp = dot(out_cols, w_out[head_rows, :]) + dot(hid[:, tail_rows], w_out[tail_rows, :])
    unp = unp.astype(BF16)
    for k in range(nx):
        up[k] = unp[k * TOK : (k + 1) * TOK]
    unp_x = [copy(up.at[(x + o) % nx], ur.at[x], xdev(o)) for o in range(1, nx)]

    for r in cot_x:
        r.wait_recv()
    pooled_grad = plg[...].reshape(rows, HEAD)
    out_grad = dot(pooled_grad, w_out[head_rows, :], ((1,), (1,))).astype(BF16)
    q_parts = []
    for p in range(rows // pair):
        ps = slice(p * pair, (p + 1) * pair)
        q_row = []
        for h in range(2):
            hs = slice(h * HEAD, (h + 1) * HEAD)
            q, v, prob = queries[ps, hs], values[ps, hs], probs[p, h]
            prob_grad = dot(out_grad[ps, hs], v, ((1,), (1,)))
            inner = jnp.sum(prob_grad * prob, axis=1, keepdims=True)
            score_grad = (prob * (prob_grad - inner) * scale).astype(BF16)
            q_row.append((dot(score_grad, q) + dot(score_grad, q, ((0,), (0,)))).astype(BF16))
        q_parts.append(jnp.concatenate(q_row, axis=1))
    q_grad = jnp.concatenate(q_parts, axis=0)

    grad_b = []
    for zk in range(2):
        for yk in range(ny):
            k = yk * 2 + zk
            term = dot(hid[:, 2 * TOK * k : 2 * TOK * (k + 1)], q_grad, ((0,), (0,))).astype(BF16)
            for ck in range(2):
                ga[ck, yk, zk] = term[TOK * ck : TOK * (ck + 1), :HEAD]
                for q in range(nzh):
                    at = TOK * ck + quarter * q
                    gb[ck, zk, q, yk] = term[at : at + quarter, HEAD:]
        grad_b.append(copy(gb.at[1 - c, zk], gcb.at[zk], core))
    grad_a = copy(ga.at[1 - c], gca, core)

    sums = up[x].astype(F32)
    for o, r in enumerate(unp_x):
        r.wait_recv()
        sums = sums + ur[(x + nx - o - 1) % nx].astype(F32)
    ub[y, zc] = sums.astype(BF16)
    unp_y = [copy(ub.at[y, zc], ub.at[y, zc], ydev(o)) for o in range(1, ny)]

    for zk in range(2):
        grad_b[zk].wait_recv()
        for q in range(nzh):
            gsb[zk, q] = (gb[c, zk, q].astype(F32) + gcb[zk, q].astype(F32)).astype(BF16)
    gb_z = [copy(gsb.at[zslot(o)], gzb.at[zz], zdev(o)) for o in range(1, nz)]
    grad_a.wait_recv()
    for k in range(ny):
        gsa[k] = (ga[c, k].astype(F32) + gca[k].astype(F32)).astype(BF16)
    ga_y = [copy(gsa.at[(y + o) % ny], gya.at[y], ydev(o)) for o in range(1, ny)]

    for r in unp_y:
        r.wait_recv()
    unp_z = copy(ub.at[:, zc], ub.at[:, zc], zpair)
    unp_c1 = copy(ub.at[:, zc], ub.at[:, zc], core)

    sums = gsb[z, zh].astype(F32)
    for o, r in enumerate(gb_z):
        r.wait_recv()
        sums = sums + gzb[(zz + nz - o - 1) % nz].astype(F32)
    rb[...] = sums.astype(BF16)
    qb_y = [copy(rb.at[(y + o) % ny], qb.at[y], ydev(o)) for o in range(1, ny)]
    sums = gsa[y].astype(F32)
    for o, r in enumerate(ga_y):
        r.wait_recv()
        sums = sums + gya[(y + ny - o - 1) % ny].astype(F32)
    for zk in range(2):
        for q in range(nzh):
            ra[zk, q] = sums[zk, quarter * q : quarter * (q + 1)].astype(BF16)
    qa_z = [copy(ra.at[zslot(o)], qa.at[zz], zdev(o)) for o in range(1, nz)]

    unp_z.wait_recv()
    unp_c2 = copy(ub.at[:, zc_far], ub.at[:, zc_far], core)

    sums = rb[y].astype(F32)
    for o, r in enumerate(qb_y):
        r.wait_recv()
        sums = sums + qb[(y + ny - o - 1) % ny].astype(F32)
    fx[x, zh, :, HEAD : 2 * HEAD] = sums.astype(BF16)
    sums = ra[z, zh].astype(F32)
    for o, r in enumerate(qa_z):
        r.wait_recv()
        sums = sums + qa[(zz + nz - o - 1) % nz].astype(F32)
    fx[x, zh, :, 0:HEAD] = sums.astype(BF16)
    fin = [copy(fx.at[x, zh], fx.at[x, zh], xzdev(ox, oz)) for ox, oz in xz]

    unp_c1.wait_recv()
    unp_c2.wait_recv()
    stores = []
    per = nb // 4
    for b in range(nb):
        owner = owners[b]
        member = (iota((TOK, BLOCK), 0) == clusters[b : b + 1, :]).astype(F32).astype(BF16)
        picked = dot(member, ub[owner // 4, owner % 4], ((0,), (0,)))
        ob[b] = (fv[b].astype(F32) + picked).astype(BF16)
        if b % per == per - 1:
            span = pl.ds(b + 1 - per, per)
            r = pltpu.make_async_copy(ob.at[span], p_out.at[span], here.at[6 + b // per])
            r.start()
            stores.append(r)

    for r in fin:
        r.wait_recv()
    for k in range(nx):
        fin_out[:, cols * k : cols * (k + 1)] = fx[k].reshape(TOK, cols).astype(F32)
    for r in stores:
        r.wait()
    for r in used:
        r.wait_send()


def layer(owners, first, last, clusters, w, tok, w_in, w_out, feat, cot, nzh, ny):
    nx, nz = NX, 2 * nzh
    d = w_in.shape[1]
    cols = 2 * HEAD
    quarter = TOK // nzh
    nb = owners.shape[0]
    n_sem = 20 + 9 * (ny - 1) + 4 * (nx - 1) + 2 * (nz - 1) + nx * nzh
    v = lambda *shape: pltpu.VMEM(shape, BF16)
    vf = lambda *shape: pltpu.VMEM(shape, F32)
    half = (2, ny, TOK, HEAD)
    side = (ny, TOK, HEAD)
    scratch = [
        v(nb, BLOCK, HEAD), v(nb, BLOCK, HEAD), v(*w_in.shape), v(*w_out.shape),
        v(nb, BLOCK, HEAD), vf(ny, 8, HEAD),
        v(*half), v(*half), v(*half), v(*half), vf(*half), vf(*half),
        v(*side), v(*side), v(*side), v(*side), v(*side), v(*side), v(*side), v(*side),
        vf(ny, 8, HEAD), vf(8, HEAD), vf(8, HEAD), vf(8, HEAD), vf(8, HEAD),
        v(ny, 4, TOK, cols), v(nx, TOK, d), v(nx, TOK, HEAD), v(nx, TOK, HEAD), v(nx * TOK, d),
        v(nx, TOK, HEAD), v(nx, TOK, HEAD), v(ny, 4, TOK, HEAD),
        v(2, ny, 2, TOK, HEAD), v(2, 2, nzh, ny, quarter, HEAD),
        v(ny, 2, TOK, HEAD), v(2, nzh, ny, quarter, HEAD),
        v(ny, 2, TOK, HEAD), v(2, nzh, ny, quarter, HEAD),
        v(ny, 2, TOK, HEAD), v(nz, ny, quarter, HEAD),
        v(2, nzh, quarter, HEAD), v(ny, quarter, HEAD), v(nz, quarter, HEAD), v(ny, quarter, HEAD),
        v(nx, nzh, quarter, cols),
        pltpu.SemaphoreType.DMA((n_sem,)), pltpu.SemaphoreType.DMA((n_sem,)),
        pltpu.SemaphoreType.DMA((10,)),
    ]
    vmem = pl.BlockSpec(memory_space=pltpu.VMEM)
    smem = pl.BlockSpec(memory_space=pltpu.SMEM)
    hbm = pl.BlockSpec(memory_space=pl.ANY)
    return pl.pallas_call(
        functools.partial(layer_kernel, nx, nzh, ny, n_sem),
        out_shape=(
            jax.ShapeDtypeStruct((nb, BLOCK, HEAD), BF16),
            jax.ShapeDtypeStruct((TOK, nx * cols), F32),
        ),
        in_specs=[smem, smem, smem, vmem] + [hbm] * 6,
        out_specs=(hbm, vmem),
        scratch_shapes=scratch,
        compiler_params=pltpu.CompilerParams(collective_id=0, has_side_effects=True),
    )(owners, first, last, clusters, w, tok, w_in, w_out, feat, cot)


def local(tokens, w_qk, w_in, w_out, particles, cotangent, clusters, owners):
    n_shard = lax.axis_size("shard")
    nzh = lax.axis_size("group") // NX
    nb = owners.shape[0]
    ids = (n_shard, nb)
    at = iota(ids, 1)
    named = jnp.broadcast_to(owners[None, :], ids) == iota(ids, 0)
    first = jnp.min(jnp.where(named, at, nb), axis=1)
    last = jnp.max(jnp.where(named, at, -1), axis=1)
    feat = particles.reshape(nb, BLOCK, -1)
    cot = cotangent.reshape(nb, BLOCK, -1)
    out, qk_grad = layer(
        owners, first, last, clusters.reshape(nb, BLOCK), w_qk, tokens, w_in, w_out, feat, cot,
        nzh, n_shard // 4,
    )
    return (out.reshape(particles.shape), qk_grad)


def solution(mesh):
    placed = (
        P(("group", "shard"), None),
        P("shard", None),
        P(),
        P(),
        P(("group", "shard"), None),
        P(("group", "shard"), None),
        P(("group", "shard")),
        P(("group", "shard")),
    )
    return jax.shard_map(
        local,
        mesh=mesh,
        in_specs=placed,
        out_specs=(P(("group", "shard"), None), P("shard", None)),
        check_vma=False,
    )
```

```python
import functools
import math

import jax
import jax.numpy as jnp
from jax import lax
from jax.experimental import pallas as pl
from jax.experimental.pallas import tpu as pltpu
from jax.sharding import PartitionSpec as P

NX = 4
HEAD = 128
TOK = 64
BLOCK = 128
MESH = pl.DeviceIdType.MESH
F32 = jnp.float32
BF16 = jnp.bfloat16


def dot(a, b, dims=((1,), (0,))):
    return lax.dot_general(a, b, (dims, ((), ())), preferred_element_type=F32)


def iota(shape, dim):
    return lax.broadcasted_iota(jnp.int32, shape, dim)


def layer_kernel(
    nx, nzh, ny, n_sem,
    owners, first, last, clusters, w, tok, w_in_hbm, w_out_hbm, feat_hbm, cot_hbm,
    p_out, fin_out,
    fv, cv, w_in, w_out, cnt,
    pf, pg, pcf, pcg, fown, gown, fzs, fzr, gzs, gzr, fys, fyr, gys, gyr,
    cy, c1, cr, c2, cq, wb, tk, plf, plg, hid, hidt, up, ur, ub,
    ga, gb, gca, gcb, gsa, gsb, gya, gzb, ra, rb, qa, qb, fx,
    send, recv, here,
):
    g = lax.axis_index("group")
    s = lax.axis_index("shard")
    x = g // nzh
    zh = g % nzh
    y = s // 4
    z = (s // 2) % 2
    c = s % 2
    zc = s % 4
    zc_far = (1 - z) * 2 + c
    nz = 2 * nzh
    zz = zh * 2 + z
    d = hid.shape[1]
    cols = 2 * HEAD
    quarter = TOK // nzh
    nb = owners.shape[0]

    core = (g, s + 1 - 2 * c)
    zpair = (g, s + 2 - 4 * z)

    def ydev(o):
        return (g, ((y + o) % ny) * 4 + zc)

    def xdev(o):
        return (((x + o) % nx) * nzh + zh, s)

    def zslot(o):
        t = (zz + o) % nz
        return t % 2, t // 2

    def zdev(o):
        zo, zho = zslot(o)
        return (x * nzh + zho, y * 4 + zo * 2 + c)

    def xzdev(ox, oz):
        return (((x + ox) % nx) * nzh + (zh + oz) % nzh, s)

    xz = [(ox, oz) for ox in range(nx) for oz in range(nzh) if ox or oz]
    used = []

    def copy(src, dst, dev):
        i = len(used)
        assert i < n_sem
        r = pltpu.make_async_remote_copy(
            src_ref=src, dst_ref=dst, send_sem=send.at[i], recv_sem=recv.at[i],
            device_id=dev, device_id_type=MESH,
        )
        used.append(r)
        r.start()
        return r

    peers = [core] + [ydev(o) for o in range(1, ny)] + [zdev(o) for o in range(1, nz)]
    peers += [xzdev(ox, oz) for ox, oz in xz if ox]
    barrier = pltpu.get_barrier_semaphore()
    for dev in peers:
        pl.semaphore_signal(barrier, inc=1, device_id=dev, device_id_type=MESH)
    mine = pl.ds(pl.multiple_of(x * cols, cols), cols)
    loads = [
        pltpu.make_async_copy(feat_hbm, fv, here.at[0]),
        pltpu.make_async_copy(cot_hbm, cv, here.at[1]),
        pltpu.make_async_copy(w.at[:, mine], wb.at[y, zc], here.at[2]),
        pltpu.make_async_copy(tok, tk.at[x], here.at[3]),
        pltpu.make_async_copy(w_in_hbm, w_in, here.at[4]),
        pltpu.make_async_copy(w_out_hbm, w_out, here.at[5]),
    ]
    for r in loads:
        r.start()
    cnt[...] = jnp.zeros_like(cnt)
    pl.semaphore_wait(barrier, len(peers))

    w_y = [copy(w.at[:, mine], wb.at[y, zc], ydev(o)) for o in range(1, ny)]
    tok_x = [copy(tok, tk.at[x], xdev(o)) for o in range(1, nx)]

    ones = jnp.ones((8, 2 * BLOCK), BF16)

    def pooled_sum(yk, zk, ck):
        owner = yk * 4 + zk * 2 + ck
        member, feats, cots = [], [], []
        b0, b1 = first[owner], last[owner]
        for at, valid in ((jnp.minimum(b0, nb - 1), b0 < nb), (jnp.maximum(b1, 0), b1 > b0)):
            labels = jnp.where(valid, clusters[pl.ds(at, 1), :], -1)
            member.append((iota((TOK, BLOCK), 0) == labels).astype(F32).astype(BF16))
            feats.append(fv[at])
            cots.append(cv[at])
        member = jnp.concatenate(member, axis=1)
        both = jnp.concatenate(
            [jnp.concatenate(feats, axis=0), jnp.concatenate(cots, axis=0)], axis=1
        )
        cnt[yk, pl.ds(zk * 2 + ck, 1), 0:TOK] = dot(ones, member, ((1,), (1,)))[:1]
        return dot(member, both)

    loads[0].wait()
    loads[1].wait()
    for yk in range(ny):
        for zk in range(2):
            v = pooled_sum(yk, zk, 1 - c)
            pf[zk, yk] = v[:, :HEAD].astype(BF16)
            pg[zk, yk] = v[:, HEAD:].astype(BF16)
    pool_f = copy(pf, pcf, core)
    pool_g = copy(pg, pcg, core)
    for yk in range(ny):
        for zk in range(2):
            v = pooled_sum(yk, zk, c)
            fown[zk, yk] = v[:, :HEAD]
            gown[zk, yk] = v[:, HEAD:]
    counts_y = [copy(cnt.at[(y + o) % ny], cy.at[y], ydev(o)) for o in range(1, ny)]

    pool_f.wait_recv()
    for k in range(ny):
        fzs[k] = (fown[1 - z, k] + pcf[1 - z, k].astype(F32)).astype(BF16)
    feat_z = copy(fzs, fzr, zpair)
    pool_g.wait_recv()
    for k in range(ny):
        gzs[k] = (gown[1 - z, k] + pcg[1 - z, k].astype(F32)).astype(BF16)
    cot_z = copy(gzs, gzr, zpair)

    feat_z.wait_recv()
    for k in range(ny):
        fys[k] = (fown[z, k] + pcf[z, k].astype(F32) + fzr[k].astype(F32)).astype(BF16)
    feat_y = [copy(fys.at[(y + o) % ny], fyr.at[y], ydev(o)) for o in range(1, ny)]

    total = cnt[y]
    for o, r in enumerate(counts_y):
        r.wait_recv()
        total = total + cy[(y + ny - o - 1) % ny]
    c1[...] = total
    counts_c = copy(c1, cr, core)

    for r in w_y:
        r.wait_recv()
    loads[2].wait()
    low, high = pl.ds(0, ny // 2), pl.ds(ny // 2, ny // 2)
    w_z0 = copy(wb.at[low, zc], wb.at[low, zc], zdev(1))
    w_z1 = copy(wb.at[high, zc], wb.at[high, zc], zdev(nz - 1))
    w_c1 = copy(wb.at[:, zc], wb.at[:, zc], core)

    counts_c.wait_recv()
    c2[...] = c1[...] + cr[...]
    counts_z = copy(c2, cq, zpair)

    cot_z.wait_recv()
    for k in range(ny):
        gys[k] = (gown[z, k] + pcg[z, k].astype(F32) + gzr[k].astype(F32)).astype(BF16)
    cot_y = [copy(gys.at[(y + o) % ny], gyr.at[y], ydev(o)) for o in range(1, ny)]

    counts_z.wait_recv()
    count = c2[...] + cq[...]
    row = jnp.sum(jnp.where(iota(count.shape, 0) == zc, count, 0.0), axis=0, keepdims=True)
    eye = iota((TOK, HEAD), 0) == iota((TOK, HEAD), 1)
    column = jnp.sum(jnp.where(eye, jnp.broadcast_to(row, (TOK, HEAD)), 0.0), axis=1, keepdims=True)

    sums = fys[y].astype(F32)
    for o, r in enumerate(feat_y):
        r.wait_recv()
        sums = sums + fyr[(y + ny - o - 1) % ny].astype(F32)
    plf[x] = (sums / jnp.maximum(column, 1.0)).astype(BF16)
    feat_x = [copy(plf.at[x], plf.at[x], xdev(o)) for o in range(1, nx)]

    w_z0.wait_recv()
    w_c2 = copy(wb.at[low, zc_far], wb.at[low, zc_far], core)
    w_z1.wait_recv()
    w_c3 = copy(wb.at[high, zc_far], wb.at[high, zc_far], core)

    sums = gys[y].astype(F32)
    for o, r in enumerate(cot_y):
        r.wait_recv()
        sums = sums + gyr[(y + ny - o - 1) % ny].astype(F32)
    plg[x] = sums.astype(BF16)
    cot_x = [copy(plg.at[x], plg.at[x], xdev(o)) for o in range(1, nx)]

    for r in loads[3:]:
        r.wait()
    for r in tok_x:
        r.wait_recv()
    for r in feat_x:
        r.wait_recv()

    rows = nx * TOK
    pooled = plf[...].reshape(rows, HEAD)
    step = 512
    for n in range(0, d, step):
        span = slice(n, n + step)
        wide = tk[:, :, span].reshape(rows, step).astype(F32) + dot(pooled, w_in[:, span])
        hid[:, span] = wide.astype(BF16)
    w_c1.wait_recv()
    w_c2.wait_recv()
    w_c3.wait_recv()
    queries = dot(hid[...], wb[...].reshape(d, cols)).astype(BF16)
    head_rows = pl.ds(pl.multiple_of(x * cols, cols), cols)
    tail_rows = pl.ds(pl.multiple_of(nx * cols + x * cols, cols), cols)
    values = hid[:, head_rows]
    scale = 1.0 / math.sqrt(HEAD)
    pair = 2 * TOK
    ii, jj = iota((pair, pair), 0), iota((pair, pair), 1)
    same = (ii // TOK) == (jj // TOK)
    diag = ii == jj
    probs, out_parts = {}, []
    for p in range(rows // pair):
        ps = slice(p * pair, (p + 1) * pair)
        out_row = []
        for h in range(2):
            hs = slice(h * HEAD, (h + 1) * HEAD)
            q, v = queries[ps, hs], values[ps, hs]
            scores = dot(q, q, ((1,), (1,))) * scale
            scores = jnp.where(diag, -1000000000.0, scores)
            scores = jnp.where(same, scores, -jnp.inf)
            e = jnp.exp(scores - jnp.max(scores, axis=1, keepdims=True))
            prob = e / jnp.sum(e, axis=1, keepdims=True)
            probs[p, h] = prob
            attended = dot(prob.astype(BF16), v)
            out_row.append((v.astype(F32) + attended).astype(BF16))
        out_parts.append(jnp.concatenate(out_row, axis=1))
    out_cols = jnp.concatenate(out_parts, axis=0)
    unp = dot(out_cols, w_out[head_rows, :]) + dot(hid[:, tail_rows], w_out[tail_rows, :])
    unp = unp.astype(BF16)
    for k in range(nx):
        up[k] = unp[k * TOK : (k + 1) * TOK]
    unp_x = [copy(up.at[(x + o) % nx], ur.at[x], xdev(o)) for o in range(1, nx)]

    for n in range(0, d, 2 * TOK):
        hidt[n : n + 2 * TOK] = hid[:, n : n + 2 * TOK].T
    for r in cot_x:
        r.wait_recv()
    pooled_grad = plg[...].reshape(rows, HEAD)
    out_grad = dot(pooled_grad, w_out[head_rows, :], ((1,), (1,))).astype(BF16)
    q_parts = []
    for p in range(rows // pair):
        ps = slice(p * pair, (p + 1) * pair)
        q_row = []
        for h in range(2):
            hs = slice(h * HEAD, (h + 1) * HEAD)
            q, v, prob = queries[ps, hs], values[ps, hs], probs[p, h]
            prob_grad = dot(out_grad[ps, hs], v, ((1,), (1,)))
            inner = jnp.sum(prob_grad * prob, axis=1, keepdims=True)
            score_grad = (prob * (prob_grad - inner) * scale).astype(BF16)
            q_row.append((dot(score_grad, q) + dot(score_grad, q, ((0,), (0,)))).astype(BF16))
        q_parts.append(jnp.concatenate(q_row, axis=1))
    q_grad = jnp.concatenate(q_parts, axis=0)

    grad_b = []
    for zk in range(2):
        for yk in range(ny):
            k = yk * 2 + zk
            term = dot(hidt[2 * TOK * k : 2 * TOK * (k + 1)], q_grad).astype(BF16)
            for ck in range(2):
                ga[ck, yk, zk] = term[TOK * ck : TOK * (ck + 1), :HEAD]
                for q in range(nzh):
                    at = TOK * ck + quarter * q
                    gb[ck, zk, q, yk] = term[at : at + quarter, HEAD:]
        grad_b.append(copy(gb.at[1 - c, zk], gcb.at[zk], core))
    grad_a = copy(ga.at[1 - c], gca, core)

    for zk in range(2):
        grad_b[zk].wait_recv()
        for q in range(nzh):
            gsb[zk, q] = (gb[c, zk, q].astype(F32) + gcb[zk, q].astype(F32)).astype(BF16)
    gb_z = [copy(gsb.at[zslot(o)], gzb.at[zz], zdev(o)) for o in range(1, nz)]
    grad_a.wait_recv()
    for k in range(ny):
        gsa[k] = (ga[c, k].astype(F32) + gca[k].astype(F32)).astype(BF16)
    ga_y = [copy(gsa.at[(y + o) % ny], gya.at[y], ydev(o)) for o in range(1, ny)]

    sums = up[x].astype(F32)
    for o, r in enumerate(unp_x):
        r.wait_recv()
        sums = sums + ur[(x + nx - o - 1) % nx].astype(F32)
    ub[y, zc] = sums.astype(BF16)
    unp_y = [copy(ub.at[y, zc], ub.at[y, zc], ydev(o)) for o in range(1, ny)]


    sums = gsb[z, zh].astype(F32)
    for o, r in enumerate(gb_z):
        r.wait_recv()
        sums = sums + gzb[(zz + nz - o - 1) % nz].astype(F32)
    rb[...] = sums.astype(BF16)
    qb_y = [copy(rb.at[(y + o) % ny], qb.at[y], ydev(o)) for o in range(1, ny)]
    sums = gsa[y].astype(F32)
    for o, r in enumerate(ga_y):
        r.wait_recv()
        sums = sums + gya[(y + ny - o - 1) % ny].astype(F32)
    for zk in range(2):
        for q in range(nzh):
            ra[zk, q] = sums[zk, quarter * q : quarter * (q + 1)].astype(BF16)
    qa_z = [copy(ra.at[zslot(o)], qa.at[zz], zdev(o)) for o in range(1, nz)]

    for r in unp_y:
        r.wait_recv()
    unp_z = copy(ub.at[:, zc], ub.at[:, zc], zpair)
    unp_c1 = copy(ub.at[:, zc], ub.at[:, zc], core)

    sums = rb[y].astype(F32)
    for o, r in enumerate(qb_y):
        r.wait_recv()
        sums = sums + qb[(y + ny - o - 1) % ny].astype(F32)
    fx[x, zh, :, HEAD : 2 * HEAD] = sums.astype(BF16)
    sums = ra[z, zh].astype(F32)
    for o, r in enumerate(qa_z):
        r.wait_recv()
        sums = sums + qa[(zz + nz - o - 1) % nz].astype(F32)
    fx[x, zh, :, 0:HEAD] = sums.astype(BF16)
    n_early = len(used)
    fin = [copy(fx.at[x, zh], fx.at[x, zh], xzdev(ox, oz)) for ox, oz in xz]

    unp_z.wait_recv()
    unp_c2 = copy(ub.at[:, zc_far], ub.at[:, zc_far], core)

    unp_c1.wait_recv()
    unp_c2.wait_recv()
    for b in range(nb):
        owner = owners[b]
        member = (iota((TOK, BLOCK), 0) == clusters[b : b + 1, :]).astype(F32).astype(BF16)
        picked = dot(member, ub[owner // 4, owner % 4], ((0,), (0,)))
        p_out[b] = (fv[b].astype(F32) + picked).astype(BF16)

    for r in used[:n_early]:
        r.wait_send()
    for r in fin:
        r.wait_recv()
    for k in range(nx):
        fin_out[:, cols * k : cols * (k + 1)] = fx[k].reshape(TOK, cols).astype(F32)
    for r in used[n_early:]:
        r.wait_send()


def layer(owners, first, last, clusters, w, tok, w_in, w_out, feat, cot, nzh, ny):
    nx, nz = NX, 2 * nzh
    d = w_in.shape[1]
    cols = 2 * HEAD
    quarter = TOK // nzh
    nb = owners.shape[0]
    n_sem = 20 + 9 * (ny - 1) + 4 * (nx - 1) + 2 * (nz - 1) + nx * nzh
    v = lambda *shape: pltpu.VMEM(shape, BF16)
    vf = lambda *shape: pltpu.VMEM(shape, F32)
    half = (2, ny, TOK, HEAD)
    side = (ny, TOK, HEAD)
    scratch = [
        v(nb, BLOCK, HEAD), v(nb, BLOCK, HEAD), v(*w_in.shape), v(*w_out.shape),
        vf(ny, 8, HEAD),
        v(*half), v(*half), v(*half), v(*half), vf(*half), vf(*half),
        v(*side), v(*side), v(*side), v(*side), v(*side), v(*side), v(*side), v(*side),
        vf(ny, 8, HEAD), vf(8, HEAD), vf(8, HEAD), vf(8, HEAD), vf(8, HEAD),
        v(ny, 4, TOK, cols), v(nx, TOK, d), v(nx, TOK, HEAD), v(nx, TOK, HEAD), v(nx * TOK, d), v(d, nx * TOK),
        v(nx, TOK, HEAD), v(nx, TOK, HEAD), v(ny, 4, TOK, HEAD),
        v(2, ny, 2, TOK, HEAD), v(2, 2, nzh, ny, quarter, HEAD),
        v(ny, 2, TOK, HEAD), v(2, nzh, ny, quarter, HEAD),
        v(ny, 2, TOK, HEAD), v(2, nzh, ny, quarter, HEAD),
        v(ny, 2, TOK, HEAD), v(nz, ny, quarter, HEAD),
        v(2, nzh, quarter, HEAD), v(ny, quarter, HEAD), v(nz, quarter, HEAD), v(ny, quarter, HEAD),
        v(nx, nzh, quarter, cols),
        pltpu.SemaphoreType.DMA((n_sem,)), pltpu.SemaphoreType.DMA((n_sem,)),
        pltpu.SemaphoreType.DMA((6,)),
    ]
    vmem = pl.BlockSpec(memory_space=pltpu.VMEM)
    smem = pl.BlockSpec(memory_space=pltpu.SMEM)
    hbm = pl.BlockSpec(memory_space=pl.ANY)
    return pl.pallas_call(
        functools.partial(layer_kernel, nx, nzh, ny, n_sem),
        out_shape=(
            pltpu.VMEM((nb, BLOCK, HEAD), BF16),
            pltpu.VMEM((TOK, nx * cols), F32),
        ),
        in_specs=[smem, smem, smem, vmem] + [hbm] * 6,
        out_specs=(vmem, vmem),
        scratch_shapes=scratch,
        compiler_params=pltpu.CompilerParams(collective_id=0, has_side_effects=True),
    )(owners, first, last, clusters, w, tok, w_in, w_out, feat, cot)


def local(tokens, w_qk, w_in, w_out, particles, cotangent, clusters, owners):
    n_shard = lax.axis_size("shard")
    nzh = lax.axis_size("group") // NX
    nb = owners.shape[0]
    ids = (n_shard, nb)
    at = iota(ids, 1)
    named = jnp.broadcast_to(owners[None, :], ids) == iota(ids, 0)
    first = jnp.min(jnp.where(named, at, nb), axis=1)
    last = jnp.max(jnp.where(named, at, -1), axis=1)
    feat = particles.reshape(nb, BLOCK, -1)
    cot = cotangent.reshape(nb, BLOCK, -1)
    out, qk_grad = layer(
        owners, first, last, clusters.reshape(nb, BLOCK), w_qk, tokens, w_in, w_out, feat, cot,
        nzh, n_shard // 4,
    )
    return (out.reshape(particles.shape), qk_grad)


def solution(mesh):
    placed = (
        P(("group", "shard"), None),
        P("shard", None),
        P(),
        P(),
        P(("group", "shard"), None),
        P(("group", "shard"), None),
        P(("group", "shard")),
        P(("group", "shard")),
    )
    return jax.shard_map(
        local,
        mesh=mesh,
        in_specs=placed,
        out_specs=(P(("group", "shard"), None), P("shard", None)),
        check_vma=False,
    )
```

```python
import functools
import math

import jax
import jax.numpy as jnp
from jax import lax
from jax.experimental import pallas as pl
from jax.experimental.pallas import tpu as pltpu
from jax.sharding import PartitionSpec as P

NX = 4
HEAD = 128
TOK = 64
BLOCK = 128
MESH = pl.DeviceIdType.MESH
F32 = jnp.float32
BF16 = jnp.bfloat16


def dot(a, b, dims=((1,), (0,))):
    return lax.dot_general(a, b, (dims, ((), ())), preferred_element_type=F32)


def iota(shape, dim):
    return lax.broadcasted_iota(jnp.int32, shape, dim)


def layer_kernel(
    nx, nzh, ny, n_sem,
    owners_hbm, clusters_hbm, w, tok, w_in_hbm, w_out_hbm, feat_hbm, cot_hbm,
    p_out, fin_out,
    owners, owner_row, ends, ends_s, clusters, fv, cv, w_in, w_out, cnt,
    pf, pg, pcf, pcg, fown, gown, fzs, fzr, gzs, gzr, fys, fyr, gys, gyr,
    cy, c1, cr, c2, cq, wb, tk, plf, plg, hid, hidt, up, ur, ub,
    ga, gb, gca, gcb, gsa, gsb, gya, gzb, ra, rb, qa, qb, fx,
    send, recv, here,
):
    g = lax.axis_index("group")
    s = lax.axis_index("shard")
    x = g // nzh
    zh = g % nzh
    y = s // 4
    z = (s // 2) % 2
    c = s % 2
    zc = s % 4
    zc_far = (1 - z) * 2 + c
    nz = 2 * nzh
    zz = zh * 2 + z
    d = hid.shape[1]
    cols = 2 * HEAD
    quarter = TOK // nzh
    nb = fv.shape[0]

    loads = [
        pltpu.make_async_copy(feat_hbm, fv, here.at[0]),
        pltpu.make_async_copy(cot_hbm, cv, here.at[1]),
        pltpu.make_async_copy(owners_hbm, owner_row, here.at[6]),
        pltpu.make_async_copy(clusters_hbm, clusters, here.at[7]),
        pltpu.make_async_copy(owners_hbm, owners, here.at[8]),
    ]
    for r in loads[2:] + loads[:2]:
        r.start()

    core = (g, s + 1 - 2 * c)
    zpair = (g, s + 2 - 4 * z)

    def ydev(o):
        return (g, ((y + o) % ny) * 4 + zc)

    def xdev(o):
        return (((x + o) % nx) * nzh + zh, s)

    def zslot(o):
        t = (zz + o) % nz
        return t % 2, t // 2

    def zdev(o):
        zo, zho = zslot(o)
        return (x * nzh + zho, y * 4 + zo * 2 + c)

    def xzdev(ox, oz):
        return (((x + ox) % nx) * nzh + (zh + oz) % nzh, s)

    xz = [(ox, oz) for ox in range(nx) for oz in range(nzh) if ox or oz]
    used = []

    def copy(src, dst, dev):
        i = len(used)
        assert i < n_sem
        r = pltpu.make_async_remote_copy(
            src_ref=src, dst_ref=dst, send_sem=send.at[i], recv_sem=recv.at[i],
            device_id=dev, device_id_type=MESH,
        )
        used.append(r)
        r.start()
        return r

    peers = [core] + [ydev(o) for o in range(1, ny)] + [zdev(o) for o in range(1, nz)]
    peers += [xzdev(ox, oz) for ox, oz in xz if ox]
    barrier = pltpu.get_barrier_semaphore()
    for dev in peers:
        pl.semaphore_signal(barrier, inc=1, device_id=dev, device_id_type=MESH)
    mine = pl.ds(pl.multiple_of(x * cols, cols), cols)
    weights = [
        pltpu.make_async_copy(w.at[:, mine], wb.at[y, zc], here.at[2]),
        pltpu.make_async_copy(tok, tk.at[x], here.at[3]),
        pltpu.make_async_copy(w_in_hbm, w_in, here.at[4]),
        pltpu.make_async_copy(w_out_hbm, w_out, here.at[5]),
    ]
    for r in weights:
        r.start()
    loads[2].wait()
    at = iota((4 * ny, nb), 1)
    named = jnp.broadcast_to(owner_row[...], (4 * ny, nb)) == iota((4 * ny, nb), 0)
    at = at.astype(F32)
    first = jnp.min(jnp.where(named, at, float(nb)), axis=1, keepdims=True)
    last = jnp.max(jnp.where(named, at, -1.0), axis=1, keepdims=True)
    ends[0] = jnp.broadcast_to(first.astype(jnp.int32), (4 * ny, HEAD))
    ends[1] = jnp.broadcast_to(last.astype(jnp.int32), (4 * ny, HEAD))
    to_scalar = pltpu.make_async_copy(ends, ends_s, here.at[9])
    to_scalar.start()
    cnt[...] = jnp.zeros_like(cnt)
    pl.semaphore_wait(barrier, len(peers))

    w_y = [copy(w.at[:, mine], wb.at[y, zc], ydev(o)) for o in range(1, ny)]
    tok_x = [copy(tok, tk.at[x], xdev(o)) for o in range(1, nx)]

    ones = jnp.ones((8, 2 * BLOCK), BF16)

    def pooled_sum(yk, zk, ck):
        owner = yk * 4 + zk * 2 + ck
        member, feats, cots = [], [], []
        b0, b1 = ends_s[0, owner, 0], ends_s[1, owner, 0]
        for at, valid in ((b0, b0 < nb), (b1, b1 > b0)):
            at = jnp.minimum(jnp.maximum(at, 0), nb - 1)
            labels = jnp.where(valid, clusters[pl.ds(at, 1), :], -1)
            member.append((iota((TOK, BLOCK), 0) == labels).astype(F32).astype(BF16))
            feats.append(fv[at])
            cots.append(cv[at])
        member = jnp.concatenate(member, axis=1)
        both = jnp.concatenate(
            [jnp.concatenate(feats, axis=0), jnp.concatenate(cots, axis=0)], axis=1
        )
        cnt[yk, pl.ds(zk * 2 + ck, 1), 0:TOK] = dot(ones, member, ((1,), (1,)))[:1]
        return dot(member, both)

    to_scalar.wait()
    for k in (3, 4, 0, 1):
        loads[k].wait()
    for yk in range(ny):
        for zk in range(2):
            v = pooled_sum(yk, zk, 1 - c)
            pf[zk, yk] = v[:, :HEAD].astype(BF16)
            pg[zk, yk] = v[:, HEAD:].astype(BF16)
    pool_f = copy(pf, pcf, core)
    pool_g = copy(pg, pcg, core)
    for yk in range(ny):
        for zk in range(2):
            v = pooled_sum(yk, zk, c)
            fown[zk, yk] = v[:, :HEAD]
            gown[zk, yk] = v[:, HEAD:]
    counts_y = [copy(cnt.at[(y + o) % ny], cy.at[y], ydev(o)) for o in range(1, ny)]

    pool_f.wait_recv()
    for k in range(ny):
        fzs[k] = (fown[1 - z, k] + pcf[1 - z, k].astype(F32)).astype(BF16)
    feat_z = copy(fzs, fzr, zpair)
    pool_g.wait_recv()
    for k in range(ny):
        gzs[k] = (gown[1 - z, k] + pcg[1 - z, k].astype(F32)).astype(BF16)
    cot_z = copy(gzs, gzr, zpair)

    feat_z.wait_recv()
    for k in range(ny):
        fys[k] = (fown[z, k] + pcf[z, k].astype(F32) + fzr[k].astype(F32)).astype(BF16)
    feat_y = [copy(fys.at[(y + o) % ny], fyr.at[y], ydev(o)) for o in range(1, ny)]

    total = cnt[y]
    for o, r in enumerate(counts_y):
        r.wait_recv()
        total = total + cy[(y + ny - o - 1) % ny]
    c1[...] = total
    counts_c = copy(c1, cr, core)

    for r in w_y:
        r.wait_recv()
    weights[0].wait()
    low, high = pl.ds(0, ny // 2), pl.ds(ny // 2, ny // 2)
    w_z0 = copy(wb.at[low, zc], wb.at[low, zc], zdev(1))
    w_z1 = copy(wb.at[high, zc], wb.at[high, zc], zdev(nz - 1))
    w_c1 = copy(wb.at[:, zc], wb.at[:, zc], core)

    counts_c.wait_recv()
    c2[...] = c1[...] + cr[...]
    counts_z = copy(c2, cq, zpair)

    cot_z.wait_recv()
    for k in range(ny):
        gys[k] = (gown[z, k] + pcg[z, k].astype(F32) + gzr[k].astype(F32)).astype(BF16)
    cot_y = [copy(gys.at[(y + o) % ny], gyr.at[y], ydev(o)) for o in range(1, ny)]

    counts_z.wait_recv()
    count = c2[...] + cq[...]
    row = jnp.sum(jnp.where(iota(count.shape, 0) == zc, count, 0.0), axis=0, keepdims=True)
    eye = iota((TOK, HEAD), 0) == iota((TOK, HEAD), 1)
    column = jnp.sum(jnp.where(eye, jnp.broadcast_to(row, (TOK, HEAD)), 0.0), axis=1, keepdims=True)

    sums = fys[y].astype(F32)
    for o, r in enumerate(feat_y):
        r.wait_recv()
        sums = sums + fyr[(y + ny - o - 1) % ny].astype(F32)
    plf[x] = (sums / jnp.maximum(column, 1.0)).astype(BF16)
    feat_x = [copy(plf.at[x], plf.at[x], xdev(o)) for o in range(1, nx)]

    w_z0.wait_recv()
    w_c2 = copy(wb.at[low, zc_far], wb.at[low, zc_far], core)
    w_z1.wait_recv()
    w_c3 = copy(wb.at[high, zc_far], wb.at[high, zc_far], core)

    sums = gys[y].astype(F32)
    for o, r in enumerate(cot_y):
        r.wait_recv()
        sums = sums + gyr[(y + ny - o - 1) % ny].astype(F32)
    plg[x] = sums.astype(BF16)
    cot_x = [copy(plg.at[x], plg.at[x], xdev(o)) for o in range(1, nx)]

    for r in weights[1:]:
        r.wait()
    for r in tok_x:
        r.wait_recv()
    for r in feat_x:
        r.wait_recv()

    rows = nx * TOK
    pooled = plf[...].reshape(rows, HEAD)
    step = 512
    for n in range(0, d, step):
        span = slice(n, n + step)
        wide = tk[:, :, span].reshape(rows, step).astype(F32) + dot(pooled, w_in[:, span])
        hid[:, span] = wide.astype(BF16)
    w_c1.wait_recv()
    w_c2.wait_recv()
    w_c3.wait_recv()
    queries = dot(hid[...], wb[...].reshape(d, cols)).astype(BF16)
    head_rows = pl.ds(pl.multiple_of(x * cols, cols), cols)
    tail_rows = pl.ds(pl.multiple_of(nx * cols + x * cols, cols), cols)
    values = hid[:, head_rows]
    scale = 1.0 / math.sqrt(HEAD)
    pair = 2 * TOK
    ii, jj = iota((pair, pair), 0), iota((pair, pair), 1)
    same = (ii // TOK) == (jj // TOK)
    diag = ii == jj
    probs, out_parts = {}, []
    for p in range(rows // pair):
        ps = slice(p * pair, (p + 1) * pair)
        out_row = []
        for h in range(2):
            hs = slice(h * HEAD, (h + 1) * HEAD)
            q, v = queries[ps, hs], values[ps, hs]
            scores = dot(q, q, ((1,), (1,))) * scale
            scores = jnp.where(diag, -1000000000.0, scores)
            scores = jnp.where(same, scores, -jnp.inf)
            e = jnp.exp(scores - jnp.max(scores, axis=1, keepdims=True))
            prob = e / jnp.sum(e, axis=1, keepdims=True)
            probs[p, h] = prob
            attended = dot(prob.astype(BF16), v)
            out_row.append((v.astype(F32) + attended).astype(BF16))
        out_parts.append(jnp.concatenate(out_row, axis=1))
    out_cols = jnp.concatenate(out_parts, axis=0)
    unp = dot(out_cols, w_out[head_rows, :]) + dot(hid[:, tail_rows], w_out[tail_rows, :])
    unp = unp.astype(BF16)
    for k in range(nx):
        up[k] = unp[k * TOK : (k + 1) * TOK]
    unp_x = [copy(up.at[(x + o) % nx], ur.at[x], xdev(o)) for o in range(1, nx)]

    for n in range(0, d, 2 * TOK):
        hidt[n : n + 2 * TOK] = hid[:, n : n + 2 * TOK].T
    for r in cot_x:
        r.wait_recv()
    pooled_grad = plg[...].reshape(rows, HEAD)
    out_grad = dot(pooled_grad, w_out[head_rows, :], ((1,), (1,))).astype(BF16)
    q_parts = []
    for p in range(rows // pair):
        ps = slice(p * pair, (p + 1) * pair)
        q_row = []
        for h in range(2):
            hs = slice(h * HEAD, (h + 1) * HEAD)
            q, v, prob = queries[ps, hs], values[ps, hs], probs[p, h]
            prob_grad = dot(out_grad[ps, hs], v, ((1,), (1,)))
            inner = jnp.sum(prob_grad * prob, axis=1, keepdims=True)
            score_grad = (prob * (prob_grad - inner) * scale).astype(BF16)
            q_row.append((dot(score_grad, q) + dot(score_grad, q, ((0,), (0,)))).astype(BF16))
        q_parts.append(jnp.concatenate(q_row, axis=1))
    q_grad = jnp.concatenate(q_parts, axis=0)

    grad_b = []
    for zk in range(2):
        for yk in range(ny):
            k = yk * 2 + zk
            term = dot(hidt[2 * TOK * k : 2 * TOK * (k + 1)], q_grad).astype(BF16)
            for ck in range(2):
                ga[ck, yk, zk] = term[TOK * ck : TOK * (ck + 1), :HEAD]
                for q in range(nzh):
                    at = TOK * ck + quarter * q
                    gb[ck, zk, q, yk] = term[at : at + quarter, HEAD:]
        grad_b.append(copy(gb.at[1 - c, zk], gcb.at[zk], core))
    grad_a = copy(ga.at[1 - c], gca, core)

    for zk in range(2):
        grad_b[zk].wait_recv()
        for q in range(nzh):
            gsb[zk, q] = (gb[c, zk, q].astype(F32) + gcb[zk, q].astype(F32)).astype(BF16)
    gb_z = [copy(gsb.at[zslot(o)], gzb.at[zz], zdev(o)) for o in range(1, nz)]
    grad_a.wait_recv()
    for k in range(ny):
        gsa[k] = (ga[c, k].astype(F32) + gca[k].astype(F32)).astype(BF16)
    ga_y = [copy(gsa.at[(y + o) % ny], gya.at[y], ydev(o)) for o in range(1, ny)]

    sums = up[x].astype(F32)
    for o, r in enumerate(unp_x):
        r.wait_recv()
        sums = sums + ur[(x + nx - o - 1) % nx].astype(F32)
    ub[y, zc] = sums.astype(BF16)
    unp_y = [copy(ub.at[y, zc], ub.at[y, zc], ydev(o)) for o in range(1, ny)]


    sums = gsb[z, zh].astype(F32)
    for o, r in enumerate(gb_z):
        r.wait_recv()
        sums = sums + gzb[(zz + nz - o - 1) % nz].astype(F32)
    rb[...] = sums.astype(BF16)
    qb_y = [copy(rb.at[(y + o) % ny], qb.at[y], ydev(o)) for o in range(1, ny)]
    sums = gsa[y].astype(F32)
    for o, r in enumerate(ga_y):
        r.wait_recv()
        sums = sums + gya[(y + ny - o - 1) % ny].astype(F32)
    for zk in range(2):
        for q in range(nzh):
            ra[zk, q] = sums[zk, quarter * q : quarter * (q + 1)].astype(BF16)
    qa_z = [copy(ra.at[zslot(o)], qa.at[zz], zdev(o)) for o in range(1, nz)]

    for r in unp_y:
        r.wait_recv()
    unp_z = copy(ub.at[:, zc], ub.at[:, zc], zpair)
    unp_c1 = copy(ub.at[:, zc], ub.at[:, zc], core)

    sums = rb[y].astype(F32)
    for o, r in enumerate(qb_y):
        r.wait_recv()
        sums = sums + qb[(y + ny - o - 1) % ny].astype(F32)
    fx[x, zh, :, HEAD : 2 * HEAD] = sums.astype(BF16)
    sums = ra[z, zh].astype(F32)
    for o, r in enumerate(qa_z):
        r.wait_recv()
        sums = sums + qa[(zz + nz - o - 1) % nz].astype(F32)
    fx[x, zh, :, 0:HEAD] = sums.astype(BF16)
    n_early = len(used)
    fin = [copy(fx.at[x, zh], fx.at[x, zh], xzdev(ox, oz)) for ox, oz in xz]

    unp_z.wait_recv()
    unp_c2 = copy(ub.at[:, zc_far], ub.at[:, zc_far], core)

    unp_c1.wait_recv()
    unp_c2.wait_recv()
    for b in range(nb):
        owner = owners[0, b]
        member = (iota((TOK, BLOCK), 0) == clusters[b : b + 1, :]).astype(F32).astype(BF16)
        picked = dot(member, ub[owner // 4, owner % 4], ((0,), (0,)))
        p_out[b] = (fv[b].astype(F32) + picked).astype(BF16)

    for r in used[:n_early]:
        r.wait_send()
    for r in fin:
        r.wait_recv()
    for k in range(nx):
        fin_out[:, cols * k : cols * (k + 1)] = fx[k].reshape(TOK, cols).astype(F32)
    for r in used[n_early:]:
        r.wait_send()


def layer(owners, clusters, w, tok, w_in, w_out, feat, cot, nzh, ny):
    nx, nz = NX, 2 * nzh
    d = w_in.shape[1]
    cols = 2 * HEAD
    quarter = TOK // nzh
    nb = clusters.shape[0]
    n_sem = 20 + 9 * (ny - 1) + 4 * (nx - 1) + 2 * (nz - 1) + nx * nzh
    v = lambda *shape: pltpu.VMEM(shape, BF16)
    vf = lambda *shape: pltpu.VMEM(shape, F32)
    half = (2, ny, TOK, HEAD)
    side = (ny, TOK, HEAD)
    scratch = [
        pltpu.SMEM((1, nb), jnp.int32), pltpu.VMEM((1, nb), jnp.int32),
        pltpu.VMEM((2, 4 * ny, HEAD), jnp.int32), pltpu.SMEM((2, 4 * ny, HEAD), jnp.int32),
        pltpu.VMEM(clusters.shape, jnp.int32),
        v(nb, BLOCK, HEAD), v(nb, BLOCK, HEAD), v(*w_in.shape), v(*w_out.shape),
        vf(ny, 8, HEAD),
        v(*half), v(*half), v(*half), v(*half), vf(*half), vf(*half),
        v(*side), v(*side), v(*side), v(*side), v(*side), v(*side), v(*side), v(*side),
        vf(ny, 8, HEAD), vf(8, HEAD), vf(8, HEAD), vf(8, HEAD), vf(8, HEAD),
        v(ny, 4, TOK, cols), v(nx, TOK, d), v(nx, TOK, HEAD), v(nx, TOK, HEAD), v(nx * TOK, d), v(d, nx * TOK),
        v(nx, TOK, HEAD), v(nx, TOK, HEAD), v(ny, 4, TOK, HEAD),
        v(2, ny, 2, TOK, HEAD), v(2, 2, nzh, ny, quarter, HEAD),
        v(ny, 2, TOK, HEAD), v(2, nzh, ny, quarter, HEAD),
        v(ny, 2, TOK, HEAD), v(2, nzh, ny, quarter, HEAD),
        v(ny, 2, TOK, HEAD), v(nz, ny, quarter, HEAD),
        v(2, nzh, quarter, HEAD), v(ny, quarter, HEAD), v(nz, quarter, HEAD), v(ny, quarter, HEAD),
        v(nx, nzh, quarter, cols),
        pltpu.SemaphoreType.DMA((n_sem,)), pltpu.SemaphoreType.DMA((n_sem,)),
        pltpu.SemaphoreType.DMA((10,)),
    ]
    vmem = pl.BlockSpec(memory_space=pltpu.VMEM)
    hbm = pl.BlockSpec(memory_space=pl.ANY)
    return pl.pallas_call(
        functools.partial(layer_kernel, nx, nzh, ny, n_sem),
        out_shape=(
            pltpu.VMEM((nb, BLOCK, HEAD), BF16),
            pltpu.VMEM((TOK, nx * cols), F32),
        ),
        in_specs=[hbm] * 8,
        out_specs=(vmem, vmem),
        scratch_shapes=scratch,
        compiler_params=pltpu.CompilerParams(collective_id=0, has_side_effects=True),
    )(owners, clusters, w, tok, w_in, w_out, feat, cot)


def place_kernel(p_in, q_in, p_out, q_out, sems):
    copies = [
        pltpu.make_async_copy(p_in, p_out, sems.at[0]),
        pltpu.make_async_copy(q_in, q_out, sems.at[1]),
    ]
    for r in copies:
        r.start()
    for r in copies:
        r.wait()


def place(p, q):
    hbm = pl.BlockSpec(memory_space=pl.ANY)
    return pl.pallas_call(
        place_kernel,
        out_shape=(jax.ShapeDtypeStruct(p.shape, p.dtype), jax.ShapeDtypeStruct(q.shape, q.dtype)),
        in_specs=[pl.BlockSpec(memory_space=pltpu.VMEM)] * 2,
        out_specs=(hbm, hbm),
        scratch_shapes=[pltpu.SemaphoreType.DMA((2,))],
    )(*(pltpu.with_memory_space_constraint(v, pltpu.VMEM) for v in (p, q)))


def local(tokens, w_qk, w_in, w_out, particles, cotangent, clusters, owners):
    n_shard = lax.axis_size("shard")
    nzh = lax.axis_size("group") // NX
    nb = owners.shape[0]
    feat = particles.reshape(nb, BLOCK, -1)
    cot = cotangent.reshape(nb, BLOCK, -1)
    out, qk_grad = layer(
        owners.reshape(1, nb), clusters.reshape(nb, BLOCK), w_qk, tokens, w_in, w_out, feat, cot,
        nzh, n_shard // 4,
    )
    out, qk_grad = place(out, qk_grad)
    return (out.reshape(particles.shape), qk_grad)


def solution(mesh):
    placed = (
        P(("group", "shard"), None),
        P("shard", None),
        P(),
        P(),
        P(("group", "shard"), None),
        P(("group", "shard"), None),
        P(("group", "shard")),
        P(("group", "shard")),
    )
    return jax.shard_map(
        local,
        mesh=mesh,
        in_specs=placed,
        out_specs=(P(("group", "shard"), None), P("shard", None)),
        check_vma=False,
    )
```

```python
import functools
import math

import jax
import jax.numpy as jnp
from jax import lax
from jax.experimental import pallas as pl
from jax.experimental.pallas import tpu as pltpu
from jax.sharding import PartitionSpec as P

NX = 4
HEAD = 128
TOK = 64
BLOCK = 128
MESH = pl.DeviceIdType.MESH
F32 = jnp.float32
BF16 = jnp.bfloat16


def dot(a, b, dims=((1,), (0,))):
    return lax.dot_general(a, b, (dims, ((), ())), preferred_element_type=F32)


def iota(shape, dim):
    return lax.broadcasted_iota(jnp.int32, shape, dim)


def far(n):
    return sorted(range(1, n), key=lambda o: -min(o, n - o))


def layer_kernel(
    nx, nzh, ny, n_sem,
    owners_hbm, clusters_hbm, w, tok, w_in_hbm, w_out_hbm, feat_hbm, cot_hbm,
    p_out, fin_out,
    owners, owner_row, ends, ends_s, clusters, fv, cv, w_in, w_out, cnt,
    pf, pg, pcf, pcg, fown, gown, fzs, fzr, gzs, gzr, fys, fyr, gys, gyr,
    cy, c1, cr, c2, cq, wb, tk, plf, plg, hid, hidt, up, ur, ub,
    ga, gb, gca, gcb, gsa, gsb, gya, gzb, ra, rb, qa, qb, fx,
    send, recv, here,
):
    g = lax.axis_index("group")
    s = lax.axis_index("shard")
    x = g // nzh
    zh = g % nzh
    y = s // 4
    z = (s // 2) % 2
    c = s % 2
    zc = s % 4
    zc_far = (1 - z) * 2 + c
    nz = 2 * nzh
    zz = zh * 2 + z
    d = hid.shape[1]
    cols = 2 * HEAD
    quarter = TOK // nzh
    nb = fv.shape[0]

    loads = [
        pltpu.make_async_copy(feat_hbm, fv, here.at[0]),
        pltpu.make_async_copy(cot_hbm, cv, here.at[1]),
        pltpu.make_async_copy(owners_hbm, owner_row, here.at[6]),
        pltpu.make_async_copy(clusters_hbm, clusters, here.at[7]),
        pltpu.make_async_copy(owners_hbm, owners, here.at[8]),
    ]
    for r in loads[2:] + loads[:2]:
        r.start()

    core = (g, s + 1 - 2 * c)
    zpair = (g, s + 2 - 4 * z)

    def ydev(o):
        return (g, ((y + o) % ny) * 4 + zc)

    def xdev(o):
        return (((x + o) % nx) * nzh + zh, s)

    def zslot(o):
        t = (zz + o) % nz
        return t % 2, t // 2

    def zdev(o):
        zo, zho = zslot(o)
        return (x * nzh + zho, y * 4 + zo * 2 + c)

    def xzdev(ox, oz):
        return (((x + ox) % nx) * nzh + (zh + oz) % nzh, s)

    xz = [(ox, oz) for ox in range(nx) for oz in range(nzh) if ox or oz]
    xz.sort(key=lambda o: -min(o[0], nx - o[0]) - 2 * min(o[1], nzh - o[1]))
    used = []

    def copy(src, dst, dev):
        i = len(used)
        assert i < n_sem
        r = pltpu.make_async_remote_copy(
            src_ref=src, dst_ref=dst, send_sem=send.at[i], recv_sem=recv.at[i],
            device_id=dev, device_id_type=MESH,
        )
        used.append(r)
        r.start()
        return r

    peers = [core] + [ydev(o) for o in range(1, ny)] + [zdev(o) for o in range(1, nz)]
    peers += [xzdev(ox, oz) for ox, oz in xz if ox]
    barrier = pltpu.get_barrier_semaphore()
    for dev in peers:
        pl.semaphore_signal(barrier, inc=1, device_id=dev, device_id_type=MESH)
    mine = pl.ds(pl.multiple_of(x * cols, cols), cols)
    weights = [
        pltpu.make_async_copy(w.at[:, mine], wb.at[y, zc], here.at[2]),
        pltpu.make_async_copy(tok, tk.at[x], here.at[3]),
        pltpu.make_async_copy(w_in_hbm, w_in, here.at[4]),
        pltpu.make_async_copy(w_out_hbm, w_out, here.at[5]),
    ]
    for r in weights:
        r.start()
    loads[2].wait()
    at = iota((4 * ny, nb), 1)
    named = jnp.broadcast_to(owner_row[...], (4 * ny, nb)) == iota((4 * ny, nb), 0)
    at = at.astype(F32)
    first = jnp.min(jnp.where(named, at, float(nb)), axis=1, keepdims=True)
    last = jnp.max(jnp.where(named, at, -1.0), axis=1, keepdims=True)
    ends[0] = jnp.broadcast_to(first.astype(jnp.int32), (4 * ny, HEAD))
    ends[1] = jnp.broadcast_to(last.astype(jnp.int32), (4 * ny, HEAD))
    to_scalar = pltpu.make_async_copy(ends, ends_s, here.at[9])
    to_scalar.start()
    cnt[...] = jnp.zeros_like(cnt)
    pl.semaphore_wait(barrier, len(peers))

    w_y = [copy(w.at[:, mine], wb.at[y, zc], ydev(o)) for o in far(ny)]
    tok_x = [copy(tok, tk.at[x], xdev(o)) for o in far(nx)]

    ones = jnp.ones((8, 2 * BLOCK), BF16)

    def pooled_sum(yk, zk, ck):
        owner = yk * 4 + zk * 2 + ck
        member, feats, cots = [], [], []
        b0, b1 = ends_s[0, owner, 0], ends_s[1, owner, 0]
        for at, valid in ((b0, b0 < nb), (b1, b1 > b0)):
            at = jnp.minimum(jnp.maximum(at, 0), nb - 1)
            labels = jnp.where(valid, clusters[pl.ds(at, 1), :], -1)
            member.append((iota((TOK, BLOCK), 0) == labels).astype(F32).astype(BF16))
            feats.append(fv[at])
            cots.append(cv[at])
        member = jnp.concatenate(member, axis=1)
        both = jnp.concatenate(
            [jnp.concatenate(feats, axis=0), jnp.concatenate(cots, axis=0)], axis=1
        )
        cnt[yk, pl.ds(zk * 2 + ck, 1), 0:TOK] = dot(ones, member, ((1,), (1,)))[:1]
        return dot(member, both)

    to_scalar.wait()
    for k in (3, 4, 0, 1):
        loads[k].wait()
    pool_f = {}
    for zk in (1 - z, z):
        for yk in range(ny):
            v = pooled_sum(yk, zk, 1 - c)
            pf[zk, yk] = v[:, :HEAD].astype(BF16)
            pg[zk, yk] = v[:, HEAD:].astype(BF16)
        pool_f[len(pool_f)] = copy(pf.at[zk], pcf.at[zk], core)
    pool_g = copy(pg, pcg, core)
    feat_z = []
    for zk in (1 - z, z):
        for yk in range(ny):
            v = pooled_sum(yk, zk, c)
            fown[zk, yk] = v[:, :HEAD]
            gown[zk, yk] = v[:, HEAD:]
        if not feat_z:
            pool_f[0].wait_recv()
            for o in far(ny) + [0]:
                k = (y + o) % ny
                fzs[k] = (fown[zk, k] + pcf[zk, k].astype(F32)).astype(BF16)
                feat_z.append(copy(fzs.at[k], fzr.at[k], zpair))
    counts_y = [copy(cnt.at[(y + o) % ny], cy.at[y], ydev(o)) for o in far(ny)]

    pool_g.wait_recv()
    for k in range(ny):
        gzs[k] = (gown[1 - z, k] + pcg[1 - z, k].astype(F32)).astype(BF16)
    cot_z = copy(gzs, gzr, zpair)

    pool_f[1].wait_recv()
    feat_y = []
    for o, r in zip(far(ny) + [0], feat_z):
        k = (y + o) % ny
        r.wait_recv()
        fys[k] = (fown[z, k] + pcf[z, k].astype(F32) + fzr[k].astype(F32)).astype(BF16)
        if o:
            feat_y.append(copy(fys.at[k], fyr.at[y], ydev(o)))

    total = cnt[y]
    for o, r in zip(far(ny), counts_y):
        r.wait_recv()
        total = total + cy[(y + ny - o) % ny]
    c1[...] = total
    counts_c = copy(c1, cr, core)

    for r in w_y:
        r.wait_recv()
    weights[0].wait()
    low, high = pl.ds(0, ny // 2), pl.ds(ny // 2, ny // 2)
    w_z0 = copy(wb.at[low, zc], wb.at[low, zc], zdev(1))
    w_z1 = copy(wb.at[high, zc], wb.at[high, zc], zdev(nz - 1))
    w_c1 = copy(wb.at[:, zc], wb.at[:, zc], core)

    counts_c.wait_recv()
    c2[...] = c1[...] + cr[...]
    counts_z = copy(c2, cq, zpair)

    cot_z.wait_recv()
    for k in range(ny):
        gys[k] = (gown[z, k] + pcg[z, k].astype(F32) + gzr[k].astype(F32)).astype(BF16)
    cot_y = [copy(gys.at[(y + o) % ny], gyr.at[y], ydev(o)) for o in far(ny)]

    counts_z.wait_recv()
    count = c2[...] + cq[...]
    row = jnp.sum(jnp.where(iota(count.shape, 0) == zc, count, 0.0), axis=0, keepdims=True)
    eye = iota((TOK, HEAD), 0) == iota((TOK, HEAD), 1)
    column = jnp.sum(jnp.where(eye, jnp.broadcast_to(row, (TOK, HEAD)), 0.0), axis=1, keepdims=True)

    sums = fys[y].astype(F32)
    for o, r in zip(far(ny), feat_y):
        r.wait_recv()
        sums = sums + fyr[(y + ny - o) % ny].astype(F32)
    plf[x] = (sums / jnp.maximum(column, 1.0)).astype(BF16)
    feat_x = [copy(plf.at[x], plf.at[x], xdev(o)) for o in far(nx)]

    w_z0.wait_recv()
    w_c2 = copy(wb.at[low, zc_far], wb.at[low, zc_far], core)
    w_z1.wait_recv()
    w_c3 = copy(wb.at[high, zc_far], wb.at[high, zc_far], core)

    sums = gys[y].astype(F32)
    for o, r in zip(far(ny), cot_y):
        r.wait_recv()
        sums = sums + gyr[(y + ny - o) % ny].astype(F32)
    plg[x] = sums.astype(BF16)
    cot_x = [copy(plg.at[x], plg.at[x], xdev(o)) for o in far(nx)]

    for r in weights[1:]:
        r.wait()
    for r in tok_x:
        r.wait_recv()
    for r in feat_x:
        r.wait_recv()

    rows = nx * TOK
    pooled = plf[...].reshape(rows, HEAD)
    step = 512
    for n in range(0, d, step):
        span = slice(n, n + step)
        wide = tk[:, :, span].reshape(rows, step).astype(F32) + dot(pooled, w_in[:, span])
        hid[:, span] = wide.astype(BF16)
    w_c1.wait_recv()
    w_c2.wait_recv()
    w_c3.wait_recv()
    queries = dot(hid[...], wb[...].reshape(d, cols)).astype(BF16)
    head_rows = pl.ds(pl.multiple_of(x * cols, cols), cols)
    tail_rows = pl.ds(pl.multiple_of(nx * cols + x * cols, cols), cols)
    values = hid[:, head_rows]
    scale = 1.0 / math.sqrt(HEAD)
    pair = 2 * TOK
    ii, jj = iota((pair, pair), 0), iota((pair, pair), 1)
    same = (ii // TOK) == (jj // TOK)
    diag = ii == jj
    probs, out_parts = {}, []
    for p in range(rows // pair):
        ps = slice(p * pair, (p + 1) * pair)
        out_row = []
        for h in range(2):
            hs = slice(h * HEAD, (h + 1) * HEAD)
            q, v = queries[ps, hs], values[ps, hs]
            scores = dot(q, q, ((1,), (1,))) * scale
            scores = jnp.where(diag, -1000000000.0, scores)
            scores = jnp.where(same, scores, -jnp.inf)
            e = jnp.exp(scores - jnp.max(scores, axis=1, keepdims=True))
            prob = e / jnp.sum(e, axis=1, keepdims=True)
            probs[p, h] = prob
            attended = dot(prob.astype(BF16), v)
            out_row.append((v.astype(F32) + attended).astype(BF16))
        out_parts.append(jnp.concatenate(out_row, axis=1))
    out_cols = jnp.concatenate(out_parts, axis=0)
    unp = dot(out_cols, w_out[head_rows, :]) + dot(hid[:, tail_rows], w_out[tail_rows, :])
    unp = unp.astype(BF16)
    for k in range(nx):
        up[k] = unp[k * TOK : (k + 1) * TOK]
    unp_x = [copy(up.at[(x + o) % nx], ur.at[x], xdev(o)) for o in far(nx)]

    for n in range(0, d, 2 * TOK):
        hidt[n : n + 2 * TOK] = hid[:, n : n + 2 * TOK].T
    for r in cot_x:
        r.wait_recv()
    pooled_grad = plg[...].reshape(rows, HEAD)
    out_grad = dot(pooled_grad, w_out[head_rows, :], ((1,), (1,))).astype(BF16)
    q_parts = []
    for p in range(rows // pair):
        ps = slice(p * pair, (p + 1) * pair)
        q_row = []
        for h in range(2):
            hs = slice(h * HEAD, (h + 1) * HEAD)
            q, v, prob = queries[ps, hs], values[ps, hs], probs[p, h]
            prob_grad = dot(out_grad[ps, hs], v, ((1,), (1,)))
            inner = jnp.sum(prob_grad * prob, axis=1, keepdims=True)
            score_grad = (prob * (prob_grad - inner) * scale).astype(BF16)
            q_row.append((dot(score_grad, q) + dot(score_grad, q, ((0,), (0,)))).astype(BF16))
        q_parts.append(jnp.concatenate(q_row, axis=1))
    q_grad = jnp.concatenate(q_parts, axis=0)

    grad_b = []
    for zk in range(2):
        for yk in range(ny):
            k = yk * 2 + zk
            term = dot(hidt[2 * TOK * k : 2 * TOK * (k + 1)], q_grad).astype(BF16)
            for ck in range(2):
                ga[ck, yk, zk] = term[TOK * ck : TOK * (ck + 1), :HEAD]
                for q in range(nzh):
                    at = TOK * ck + quarter * q
                    gb[ck, zk, q, yk] = term[at : at + quarter, HEAD:]
        grad_b.append(copy(gb.at[1 - c, zk], gcb.at[zk], core))
    grad_a = copy(ga.at[1 - c], gca, core)

    for zk in range(2):
        grad_b[zk].wait_recv()
        for q in range(nzh):
            gsb[zk, q] = (gb[c, zk, q].astype(F32) + gcb[zk, q].astype(F32)).astype(BF16)
    gb_z = [copy(gsb.at[zslot(o)], gzb.at[zz], zdev(o)) for o in far(nz)]
    grad_a.wait_recv()
    for k in range(ny):
        gsa[k] = (ga[c, k].astype(F32) + gca[k].astype(F32)).astype(BF16)
    ga_y = [copy(gsa.at[(y + o) % ny], gya.at[y], ydev(o)) for o in far(ny)]

    sums = up[x].astype(F32)
    for o, r in zip(far(nx), unp_x):
        r.wait_recv()
        sums = sums + ur[(x + nx - o) % nx].astype(F32)
    ub[y, zc] = sums.astype(BF16)
    unp_y = [copy(ub.at[y, zc], ub.at[y, zc], ydev(o)) for o in far(ny)]


    sums = gsb[z, zh].astype(F32)
    for o, r in zip(far(nz), gb_z):
        r.wait_recv()
        sums = sums + gzb[(zz + nz - o) % nz].astype(F32)
    rb[...] = sums.astype(BF16)
    qb_y = [copy(rb.at[(y + o) % ny], qb.at[y], ydev(o)) for o in far(ny)]
    sums = gsa[y].astype(F32)
    for o, r in zip(far(ny), ga_y):
        r.wait_recv()
        sums = sums + gya[(y + ny - o) % ny].astype(F32)
    for zk in range(2):
        for q in range(nzh):
            ra[zk, q] = sums[zk, quarter * q : quarter * (q + 1)].astype(BF16)
    qa_z = [copy(ra.at[zslot(o)], qa.at[zz], zdev(o)) for o in far(nz)]

    for r in unp_y:
        r.wait_recv()
    unp_z = copy(ub.at[:, zc], ub.at[:, zc], zpair)
    unp_c1 = copy(ub.at[:, zc], ub.at[:, zc], core)

    sums = rb[y].astype(F32)
    for o, r in zip(far(ny), qb_y):
        r.wait_recv()
        sums = sums + qb[(y + ny - o) % ny].astype(F32)
    fx[x, zh, :, HEAD : 2 * HEAD] = sums.astype(BF16)
    sums = ra[z, zh].astype(F32)
    for o, r in zip(far(nz), qa_z):
        r.wait_recv()
        sums = sums + qa[(zz + nz - o) % nz].astype(F32)
    fx[x, zh, :, 0:HEAD] = sums.astype(BF16)
    n_early = len(used)
    fin = [copy(fx.at[x, zh], fx.at[x, zh], xzdev(ox, oz)) for ox, oz in xz]

    unp_z.wait_recv()
    unp_c2 = copy(ub.at[:, zc_far], ub.at[:, zc_far], core)

    unp_c1.wait_recv()
    unp_c2.wait_recv()
    for b in range(nb):
        owner = owners[0, b]
        member = (iota((TOK, BLOCK), 0) == clusters[b : b + 1, :]).astype(F32).astype(BF16)
        picked = dot(member, ub[owner // 4, owner % 4], ((0,), (0,)))
        p_out[b] = (fv[b].astype(F32) + picked).astype(BF16)

    for r in used[:n_early]:
        r.wait_send()
    for r in fin:
        r.wait_recv()
    for k in range(nx):
        fin_out[:, cols * k : cols * (k + 1)] = fx[k].reshape(TOK, cols).astype(F32)
    for r in used[n_early:]:
        r.wait_send()


def layer(owners, clusters, w, tok, w_in, w_out, feat, cot, nzh, ny):
    nx, nz = NX, 2 * nzh
    d = w_in.shape[1]
    cols = 2 * HEAD
    quarter = TOK // nzh
    nb = clusters.shape[0]
    n_sem = 24 + 10 * (ny - 1) + 4 * (nx - 1) + 2 * (nz - 1) + nx * nzh
    v = lambda *shape: pltpu.VMEM(shape, BF16)
    vf = lambda *shape: pltpu.VMEM(shape, F32)
    half = (2, ny, TOK, HEAD)
    side = (ny, TOK, HEAD)
    scratch = [
        pltpu.SMEM((1, nb), jnp.int32), pltpu.VMEM((1, nb), jnp.int32),
        pltpu.VMEM((2, 4 * ny, HEAD), jnp.int32), pltpu.SMEM((2, 4 * ny, HEAD), jnp.int32),
        pltpu.VMEM(clusters.shape, jnp.int32),
        v(nb, BLOCK, HEAD), v(nb, BLOCK, HEAD), v(*w_in.shape), v(*w_out.shape),
        vf(ny, 8, HEAD),
        v(*half), v(*half), v(*half), v(*half), vf(*half), vf(*half),
        v(*side), v(*side), v(*side), v(*side), v(*side), v(*side), v(*side), v(*side),
        vf(ny, 8, HEAD), vf(8, HEAD), vf(8, HEAD), vf(8, HEAD), vf(8, HEAD),
        v(ny, 4, TOK, cols), v(nx, TOK, d), v(nx, TOK, HEAD), v(nx, TOK, HEAD), v(nx * TOK, d), v(d, nx * TOK),
        v(nx, TOK, HEAD), v(nx, TOK, HEAD), v(ny, 4, TOK, HEAD),
        v(2, ny, 2, TOK, HEAD), v(2, 2, nzh, ny, quarter, HEAD),
        v(ny, 2, TOK, HEAD), v(2, nzh, ny, quarter, HEAD),
        v(ny, 2, TOK, HEAD), v(2, nzh, ny, quarter, HEAD),
        v(ny, 2, TOK, HEAD), v(nz, ny, quarter, HEAD),
        v(2, nzh, quarter, HEAD), v(ny, quarter, HEAD), v(nz, quarter, HEAD), v(ny, quarter, HEAD),
        v(nx, nzh, quarter, cols),
        pltpu.SemaphoreType.DMA((n_sem,)), pltpu.SemaphoreType.DMA((n_sem,)),
        pltpu.SemaphoreType.DMA((10,)),
    ]
    vmem = pl.BlockSpec(memory_space=pltpu.VMEM)
    hbm = pl.BlockSpec(memory_space=pl.ANY)
    return pl.pallas_call(
        functools.partial(layer_kernel, nx, nzh, ny, n_sem),
        out_shape=(
            pltpu.VMEM((nb, BLOCK, HEAD), BF16),
            pltpu.VMEM((TOK, nx * cols), F32),
        ),
        in_specs=[hbm] * 8,
        out_specs=(vmem, vmem),
        scratch_shapes=scratch,
        compiler_params=pltpu.CompilerParams(collective_id=0, has_side_effects=True),
    )(owners, clusters, w, tok, w_in, w_out, feat, cot)


def place_kernel(p_in, q_in, p_out, q_out, sems):
    copies = [
        pltpu.make_async_copy(p_in, p_out, sems.at[0]),
        pltpu.make_async_copy(q_in, q_out, sems.at[1]),
    ]
    for r in copies:
        r.start()
    for r in copies:
        r.wait()


def place(p, q):
    hbm = pl.BlockSpec(memory_space=pl.ANY)
    return pl.pallas_call(
        place_kernel,
        out_shape=(jax.ShapeDtypeStruct(p.shape, p.dtype), jax.ShapeDtypeStruct(q.shape, q.dtype)),
        in_specs=[pl.BlockSpec(memory_space=pltpu.VMEM)] * 2,
        out_specs=(hbm, hbm),
        scratch_shapes=[pltpu.SemaphoreType.DMA((2,))],
    )(*(pltpu.with_memory_space_constraint(v, pltpu.VMEM) for v in (p, q)))


def local(tokens, w_qk, w_in, w_out, particles, cotangent, clusters, owners):
    n_shard = lax.axis_size("shard")
    nzh = lax.axis_size("group") // NX
    nb = owners.shape[0]
    feat = particles.reshape(nb, BLOCK, -1)
    cot = cotangent.reshape(nb, BLOCK, -1)
    out, qk_grad = layer(
        owners.reshape(1, nb), clusters.reshape(nb, BLOCK), w_qk, tokens, w_in, w_out, feat, cot,
        nzh, n_shard // 4,
    )
    out, qk_grad = place(out, qk_grad)
    return (out.reshape(particles.shape), qk_grad)


def solution(mesh):
    placed = (
        P(("group", "shard"), None),
        P("shard", None),
        P(),
        P(),
        P(("group", "shard"), None),
        P(("group", "shard"), None),
        P(("group", "shard")),
        P(("group", "shard")),
    )
    return jax.shard_map(
        local,
        mesh=mesh,
        in_specs=placed,
        out_specs=(P(("group", "shard"), None), P("shard", None)),
        check_vma=False,
    )
```

```python
import functools
import math

import jax
import jax.numpy as jnp
from jax import lax
from jax.experimental import pallas as pl
from jax.experimental.pallas import tpu as pltpu
from jax.sharding import PartitionSpec as P

NX = 4
HEAD = 128
TOK = 64
BLOCK = 128
MESH = pl.DeviceIdType.MESH
F32 = jnp.float32
BF16 = jnp.bfloat16


def dot(a, b, dims=((1,), (0,))):
    return lax.dot_general(a, b, (dims, ((), ())), preferred_element_type=F32)


def iota(shape, dim):
    return lax.broadcasted_iota(jnp.int32, shape, dim)


def far(n):
    return sorted(range(1, n), key=lambda o: -min(o, n - o))


def layer_kernel(
    nx, nzh, ny, n_sem,
    owners_hbm, clusters_hbm, w, tok, w_in_hbm, w_out_hbm, feat_hbm, cot_hbm,
    p_out, fin_out,
    owners, owner_row, ends, ends_s, clusters, fv, cv, w_in, w_out, cnt,
    pf, pg, pcf, pcg, fown, gown, fzs, fzr, gzs, gzr, fys, fyr, gys, gyr,
    cy, c1, cr, c2, cq, wb, tk, plf, plg, hid, hidt, up, ur, ub,
    ga, gb, gca, gcb, gsa, gsb, gya, gzb, ra, rb, qa, qb, fx,
    send, recv, here,
):
    g = lax.axis_index("group")
    s = lax.axis_index("shard")
    x = g // nzh
    zh = g % nzh
    y = s // 4
    z = (s // 2) % 2
    c = s % 2
    zc = s % 4
    zc_far = (1 - z) * 2 + c
    nz = 2 * nzh
    zz = zh * 2 + z
    d = hid.shape[1]
    cols = 2 * HEAD
    quarter = TOK // nzh
    nb = fv.shape[0]

    loads = [
        pltpu.make_async_copy(feat_hbm, fv, here.at[0]),
        pltpu.make_async_copy(cot_hbm, cv, here.at[1]),
        pltpu.make_async_copy(owners_hbm, owner_row, here.at[6]),
        pltpu.make_async_copy(clusters_hbm, clusters, here.at[7]),
        pltpu.make_async_copy(owners_hbm, owners, here.at[8]),
    ]
    for r in loads[2:] + loads[:2]:
        r.start()

    core = (g, s + 1 - 2 * c)
    zpair = (g, s + 2 - 4 * z)

    def ydev(o):
        return (g, ((y + o) % ny) * 4 + zc)

    def xdev(o):
        return (((x + o) % nx) * nzh + zh, s)

    def zslot(o):
        t = (zz + o) % nz
        return t % 2, t // 2

    def zdev(o):
        zo, zho = zslot(o)
        return (x * nzh + zho, y * 4 + zo * 2 + c)

    def xzdev(ox, oz):
        return (((x + ox) % nx) * nzh + (zh + oz) % nzh, s)

    xz = [(ox, oz) for ox in range(nx) for oz in range(nzh) if ox or oz]
    xz.sort(key=lambda o: -min(o[0], nx - o[0]) - 2 * min(o[1], nzh - o[1]))
    used = []

    def copy(src, dst, dev):
        i = len(used)
        assert i < n_sem
        r = pltpu.make_async_remote_copy(
            src_ref=src, dst_ref=dst, send_sem=send.at[i], recv_sem=recv.at[i],
            device_id=dev, device_id_type=MESH,
        )
        used.append(r)
        r.start()
        return r

    peers = [core] + [ydev(o) for o in range(1, ny)] + [zdev(o) for o in range(1, nz)]
    peers += [xzdev(ox, oz) for ox, oz in xz if ox]
    barrier = pltpu.get_barrier_semaphore()
    for dev in peers:
        pl.semaphore_signal(barrier, inc=1, device_id=dev, device_id_type=MESH)
    mine = pl.ds(pl.multiple_of(x * cols, cols), cols)
    weights = [
        pltpu.make_async_copy(w.at[:, mine], wb.at[y, zc], here.at[2]),
        pltpu.make_async_copy(tok, tk.at[x], here.at[3]),
        pltpu.make_async_copy(w_in_hbm, w_in, here.at[4]),
        pltpu.make_async_copy(w_out_hbm, w_out, here.at[5]),
    ]
    for r in weights:
        r.start()
    loads[2].wait()
    at = iota((4 * ny, nb), 1)
    named = jnp.broadcast_to(owner_row[...], (4 * ny, nb)) == iota((4 * ny, nb), 0)
    at = at.astype(F32)
    first = jnp.min(jnp.where(named, at, float(nb)), axis=1, keepdims=True)
    last = jnp.max(jnp.where(named, at, -1.0), axis=1, keepdims=True)
    ends[0] = jnp.broadcast_to(first.astype(jnp.int32), (4 * ny, HEAD))
    ends[1] = jnp.broadcast_to(last.astype(jnp.int32), (4 * ny, HEAD))
    to_scalar = pltpu.make_async_copy(ends, ends_s, here.at[9])
    to_scalar.start()
    cnt[...] = jnp.zeros_like(cnt)
    pl.semaphore_wait(barrier, len(peers))

    w_y = [copy(w.at[:, mine], wb.at[y, zc], ydev(o)) for o in far(ny)]
    tok_x = [copy(tok, tk.at[x], xdev(o)) for o in far(nx)]

    ones = jnp.ones((8, 2 * BLOCK), BF16)

    def pooled_sum(yk, zk, ck):
        owner = yk * 4 + zk * 2 + ck
        member, feats, cots = [], [], []
        b0, b1 = ends_s[0, owner, 0], ends_s[1, owner, 0]
        for at, valid in ((b0, b0 < nb), (b1, b1 > b0)):
            at = jnp.minimum(jnp.maximum(at, 0), nb - 1)
            labels = jnp.where(valid, clusters[pl.ds(at, 1), :], -1)
            member.append((iota((TOK, BLOCK), 0) == labels).astype(F32).astype(BF16))
            feats.append(fv[at])
            cots.append(cv[at])
        member = jnp.concatenate(member, axis=1)
        both = jnp.concatenate(
            [jnp.concatenate(feats, axis=0), jnp.concatenate(cots, axis=0)], axis=1
        )
        cnt[yk, pl.ds(zk * 2 + ck, 1), 0:TOK] = dot(ones, member, ((1,), (1,)))[:1]
        return dot(member, both)

    to_scalar.wait()
    for k in (3, 4, 0, 1):
        loads[k].wait()
    pool_f = {}
    for zk in (1 - z, z):
        for yk in range(ny):
            v = pooled_sum(yk, zk, 1 - c)
            pf[zk, yk] = v[:, :HEAD].astype(BF16)
            pg[zk, yk] = v[:, HEAD:].astype(BF16)
        pool_f[len(pool_f)] = copy(pf.at[zk], pcf.at[zk], core)
    pool_g = copy(pg, pcg, core)
    feat_z = []
    for zk in (1 - z, z):
        for yk in range(ny):
            v = pooled_sum(yk, zk, c)
            fown[zk, yk] = v[:, :HEAD]
            gown[zk, yk] = v[:, HEAD:]
        if not feat_z:
            pool_f[0].wait_recv()
            for o in far(ny) + [0]:
                k = (y + o) % ny
                fzs[k] = (fown[zk, k] + pcf[zk, k].astype(F32)).astype(BF16)
                feat_z.append(copy(fzs.at[k], fzr.at[k], zpair))
    counts_y = [copy(cnt.at[(y + o) % ny], cy.at[y], ydev(o)) for o in far(ny)]

    pool_g.wait_recv()
    cot_z = []
    for o in far(ny) + [0]:
        k = (y + o) % ny
        gzs[k] = (gown[1 - z, k] + pcg[1 - z, k].astype(F32)).astype(BF16)
        cot_z.append(copy(gzs.at[k], gzr.at[k], zpair))

    pool_f[1].wait_recv()
    feat_y = []
    for o, r in zip(far(ny) + [0], feat_z):
        k = (y + o) % ny
        r.wait_recv()
        fys[k] = (fown[z, k] + pcf[z, k].astype(F32) + fzr[k].astype(F32)).astype(BF16)
        if o:
            feat_y.append(copy(fys.at[k], fyr.at[y], ydev(o)))

    total = cnt[y]
    for o, r in zip(far(ny), counts_y):
        r.wait_recv()
        total = total + cy[(y + ny - o) % ny]
    c1[...] = total
    counts_c = copy(c1, cr, core)

    for r in w_y:
        r.wait_recv()
    weights[0].wait()
    low, high = pl.ds(0, ny // 2), pl.ds(ny // 2, ny // 2)
    w_z0 = copy(wb.at[low, zc], wb.at[low, zc], zdev(1))
    w_z1 = copy(wb.at[high, zc], wb.at[high, zc], zdev(nz - 1))
    w_c1 = copy(wb.at[:, zc], wb.at[:, zc], core)

    counts_c.wait_recv()
    c2[...] = c1[...] + cr[...]
    counts_z = copy(c2, cq, zpair)

    cot_y = []
    for o, r in zip(far(ny) + [0], cot_z):
        k = (y + o) % ny
        r.wait_recv()
        gys[k] = (gown[z, k] + pcg[z, k].astype(F32) + gzr[k].astype(F32)).astype(BF16)
        if o:
            cot_y.append(copy(gys.at[k], gyr.at[y], ydev(o)))

    counts_z.wait_recv()
    count = c2[...] + cq[...]
    row = jnp.sum(jnp.where(iota(count.shape, 0) == zc, count, 0.0), axis=0, keepdims=True)
    eye = iota((TOK, HEAD), 0) == iota((TOK, HEAD), 1)
    column = jnp.sum(jnp.where(eye, jnp.broadcast_to(row, (TOK, HEAD)), 0.0), axis=1, keepdims=True)

    sums = fys[y].astype(F32)
    for o, r in zip(far(ny), feat_y):
        r.wait_recv()
        sums = sums + fyr[(y + ny - o) % ny].astype(F32)
    plf[x] = (sums / jnp.maximum(column, 1.0)).astype(BF16)
    feat_x = [copy(plf.at[x], plf.at[x], xdev(o)) for o in far(nx)]

    w_z0.wait_recv()
    w_c2 = copy(wb.at[low, zc_far], wb.at[low, zc_far], core)
    w_z1.wait_recv()
    w_c3 = copy(wb.at[high, zc_far], wb.at[high, zc_far], core)

    sums = gys[y].astype(F32)
    for o, r in zip(far(ny), cot_y):
        r.wait_recv()
        sums = sums + gyr[(y + ny - o) % ny].astype(F32)
    plg[x] = sums.astype(BF16)
    cot_x = [copy(plg.at[x], plg.at[x], xdev(o)) for o in far(nx)]

    for r in weights[1:]:
        r.wait()
    for r in tok_x:
        r.wait_recv()
    for r in feat_x:
        r.wait_recv()

    rows = nx * TOK
    pooled = plf[...].reshape(rows, HEAD)
    step = 512
    for n in range(0, d, step):
        span = slice(n, n + step)
        wide = tk[:, :, span].reshape(rows, step).astype(F32) + dot(pooled, w_in[:, span])
        hid[:, span] = wide.astype(BF16)
    w_c1.wait_recv()
    w_c2.wait_recv()
    w_c3.wait_recv()
    queries = dot(hid[...], wb[...].reshape(d, cols)).astype(BF16)
    head_rows = pl.ds(pl.multiple_of(x * cols, cols), cols)
    tail_rows = pl.ds(pl.multiple_of(nx * cols + x * cols, cols), cols)
    values = hid[:, head_rows]
    scale = 1.0 / math.sqrt(HEAD)
    pair = 2 * TOK
    ii, jj = iota((pair, pair), 0), iota((pair, pair), 1)
    same = (ii // TOK) == (jj // TOK)
    diag = ii == jj
    probs, out_parts = {}, []
    for p in range(rows // pair):
        ps = slice(p * pair, (p + 1) * pair)
        out_row = []
        for h in range(2):
            hs = slice(h * HEAD, (h + 1) * HEAD)
            q, v = queries[ps, hs], values[ps, hs]
            scores = dot(q, q, ((1,), (1,))) * scale
            scores = jnp.where(diag, -1000000000.0, scores)
            scores = jnp.where(same, scores, -jnp.inf)
            e = jnp.exp(scores - jnp.max(scores, axis=1, keepdims=True))
            prob = e / jnp.sum(e, axis=1, keepdims=True)
            probs[p, h] = prob
            attended = dot(prob.astype(BF16), v)
            out_row.append((v.astype(F32) + attended).astype(BF16))
        out_parts.append(jnp.concatenate(out_row, axis=1))
    out_cols = jnp.concatenate(out_parts, axis=0)
    unp = dot(out_cols, w_out[head_rows, :]) + dot(hid[:, tail_rows], w_out[tail_rows, :])
    unp = unp.astype(BF16)
    for k in range(nx):
        up[k] = unp[k * TOK : (k + 1) * TOK]
    unp_x = [copy(up.at[(x + o) % nx], ur.at[x], xdev(o)) for o in far(nx)]

    for n in range(0, d, 2 * TOK):
        hidt[n : n + 2 * TOK] = hid[:, n : n + 2 * TOK].T
    for r in cot_x:
        r.wait_recv()
    pooled_grad = plg[...].reshape(rows, HEAD)
    out_grad = dot(pooled_grad, w_out[head_rows, :], ((1,), (1,))).astype(BF16)
    q_parts = []
    for p in range(rows // pair):
        ps = slice(p * pair, (p + 1) * pair)
        q_row = []
        for h in range(2):
            hs = slice(h * HEAD, (h + 1) * HEAD)
            q, v, prob = queries[ps, hs], values[ps, hs], probs[p, h]
            prob_grad = dot(out_grad[ps, hs], v, ((1,), (1,)))
            inner = jnp.sum(prob_grad * prob, axis=1, keepdims=True)
            score_grad = (prob * (prob_grad - inner) * scale).astype(BF16)
            q_row.append((dot(score_grad, q) + dot(score_grad, q, ((0,), (0,)))).astype(BF16))
        q_parts.append(jnp.concatenate(q_row, axis=1))
    q_grad = jnp.concatenate(q_parts, axis=0)

    grad_a, grad_b = [], []
    for zk in range(2):
        for yk in range(ny):
            k = yk * 2 + zk
            term = dot(hidt[2 * TOK * k : 2 * TOK * (k + 1)], q_grad).astype(BF16)
            for ck in range(2):
                ga[ck, yk, zk] = term[TOK * ck : TOK * (ck + 1), :HEAD]
                for q in range(nzh):
                    at = TOK * ck + quarter * q
                    gb[ck, zk, q, yk] = term[at : at + quarter, HEAD:]
        grad_b.append(copy(gb.at[1 - c, zk], gcb.at[zk], core))
        grad_a.append(copy(ga.at[1 - c, :, zk], gca.at[:, zk], core))

    for zk in range(2):
        grad_b[zk].wait_recv()
        for q in range(nzh):
            gsb[zk, q] = (gb[c, zk, q].astype(F32) + gcb[zk, q].astype(F32)).astype(BF16)
    gb_z = [copy(gsb.at[zslot(o)], gzb.at[zz], zdev(o)) for o in far(nz)]
    for r in grad_a:
        r.wait_recv()
    ga_y = []
    for o in far(ny) + [0]:
        k = (y + o) % ny
        gsa[k] = (ga[c, k].astype(F32) + gca[k].astype(F32)).astype(BF16)
        if o:
            ga_y.append(copy(gsa.at[k], gya.at[y], ydev(o)))

    sums = up[x].astype(F32)
    for o, r in zip(far(nx), unp_x):
        r.wait_recv()
        sums = sums + ur[(x + nx - o) % nx].astype(F32)
    ub[y, zc] = sums.astype(BF16)
    unp_y = [copy(ub.at[y, zc], ub.at[y, zc], ydev(o)) for o in far(ny)]


    sums = gsb[z, zh].astype(F32)
    for o, r in zip(far(nz), gb_z):
        r.wait_recv()
        sums = sums + gzb[(zz + nz - o) % nz].astype(F32)
    rb[...] = sums.astype(BF16)
    qb_y = [copy(rb.at[(y + o) % ny], qb.at[y], ydev(o)) for o in far(ny)]
    sums = gsa[y].astype(F32)
    for o, r in zip(far(ny), ga_y):
        r.wait_recv()
        sums = sums + gya[(y + ny - o) % ny].astype(F32)
    for zk in range(2):
        for q in range(nzh):
            ra[zk, q] = sums[zk, quarter * q : quarter * (q + 1)].astype(BF16)
    qa_z = [copy(ra.at[zslot(o)], qa.at[zz], zdev(o)) for o in far(nz)]

    for r in unp_y:
        r.wait_recv()
    unp_z = copy(ub.at[:, zc], ub.at[:, zc], zpair)
    unp_c1 = copy(ub.at[:, zc], ub.at[:, zc], core)

    sums = rb[y].astype(F32)
    for o, r in zip(far(ny), qb_y):
        r.wait_recv()
        sums = sums + qb[(y + ny - o) % ny].astype(F32)
    fx[x, zh, :, HEAD : 2 * HEAD] = sums.astype(BF16)
    sums = ra[z, zh].astype(F32)
    for o, r in zip(far(nz), qa_z):
        r.wait_recv()
        sums = sums + qa[(zz + nz - o) % nz].astype(F32)
    fx[x, zh, :, 0:HEAD] = sums.astype(BF16)
    n_early = len(used)
    fin = [copy(fx.at[x, zh], fx.at[x, zh], xzdev(ox, oz)) for ox, oz in xz]

    unp_z.wait_recv()
    unp_c2 = copy(ub.at[:, zc_far], ub.at[:, zc_far], core)

    unp_c1.wait_recv()
    unp_c2.wait_recv()
    for b in range(nb):
        owner = owners[0, b]
        member = (iota((TOK, BLOCK), 0) == clusters[b : b + 1, :]).astype(F32).astype(BF16)
        picked = dot(member, ub[owner // 4, owner % 4], ((0,), (0,)))
        p_out[b] = (fv[b].astype(F32) + picked).astype(BF16)

    for r in used[:n_early]:
        r.wait_send()
    for r in fin:
        r.wait_recv()
    for k in range(nx):
        fin_out[:, cols * k : cols * (k + 1)] = fx[k].reshape(TOK, cols).astype(F32)
    for r in used[n_early:]:
        r.wait_send()


def layer(owners, clusters, w, tok, w_in, w_out, feat, cot, nzh, ny):
    nx, nz = NX, 2 * nzh
    d = w_in.shape[1]
    cols = 2 * HEAD
    quarter = TOK // nzh
    nb = clusters.shape[0]
    n_sem = 26 + 11 * (ny - 1) + 4 * (nx - 1) + 2 * (nz - 1) + nx * nzh
    v = lambda *shape: pltpu.VMEM(shape, BF16)
    vf = lambda *shape: pltpu.VMEM(shape, F32)
    half = (2, ny, TOK, HEAD)
    side = (ny, TOK, HEAD)
    scratch = [
        pltpu.SMEM((1, nb), jnp.int32), pltpu.VMEM((1, nb), jnp.int32),
        pltpu.VMEM((2, 4 * ny, HEAD), jnp.int32), pltpu.SMEM((2, 4 * ny, HEAD), jnp.int32),
        pltpu.VMEM(clusters.shape, jnp.int32),
        v(nb, BLOCK, HEAD), v(nb, BLOCK, HEAD), v(*w_in.shape), v(*w_out.shape),
        vf(ny, 8, HEAD),
        v(*half), v(*half), v(*half), v(*half), vf(*half), vf(*half),
        v(*side), v(*side), v(*side), v(*side), v(*side), v(*side), v(*side), v(*side),
        vf(ny, 8, HEAD), vf(8, HEAD), vf(8, HEAD), vf(8, HEAD), vf(8, HEAD),
        v(ny, 4, TOK, cols), v(nx, TOK, d), v(nx, TOK, HEAD), v(nx, TOK, HEAD), v(nx * TOK, d), v(d, nx * TOK),
        v(nx, TOK, HEAD), v(nx, TOK, HEAD), v(ny, 4, TOK, HEAD),
        v(2, ny, 2, TOK, HEAD), v(2, 2, nzh, ny, quarter, HEAD),
        v(ny, 2, TOK, HEAD), v(2, nzh, ny, quarter, HEAD),
        v(ny, 2, TOK, HEAD), v(2, nzh, ny, quarter, HEAD),
        v(ny, 2, TOK, HEAD), v(nz, ny, quarter, HEAD),
        v(2, nzh, quarter, HEAD), v(ny, quarter, HEAD), v(nz, quarter, HEAD), v(ny, quarter, HEAD),
        v(nx, nzh, quarter, cols),
        pltpu.SemaphoreType.DMA((n_sem,)), pltpu.SemaphoreType.DMA((n_sem,)),
        pltpu.SemaphoreType.DMA((10,)),
    ]
    vmem = pl.BlockSpec(memory_space=pltpu.VMEM)
    hbm = pl.BlockSpec(memory_space=pl.ANY)
    return pl.pallas_call(
        functools.partial(layer_kernel, nx, nzh, ny, n_sem),
        out_shape=(
            pltpu.VMEM((nb, BLOCK, HEAD), BF16),
            pltpu.VMEM((TOK, nx * cols), F32),
        ),
        in_specs=[hbm] * 8,
        out_specs=(vmem, vmem),
        scratch_shapes=scratch,
        compiler_params=pltpu.CompilerParams(collective_id=0, has_side_effects=True),
    )(owners, clusters, w, tok, w_in, w_out, feat, cot)


def place_kernel(p_in, q_in, p_out, q_out, sems):
    copies = [
        pltpu.make_async_copy(p_in, p_out, sems.at[0]),
        pltpu.make_async_copy(q_in, q_out, sems.at[1]),
    ]
    for r in copies:
        r.start()
    for r in copies:
        r.wait()


def place(p, q):
    hbm = pl.BlockSpec(memory_space=pl.ANY)
    return pl.pallas_call(
        place_kernel,
        out_shape=(jax.ShapeDtypeStruct(p.shape, p.dtype), jax.ShapeDtypeStruct(q.shape, q.dtype)),
        in_specs=[pl.BlockSpec(memory_space=pltpu.VMEM)] * 2,
        out_specs=(hbm, hbm),
        scratch_shapes=[pltpu.SemaphoreType.DMA((2,))],
    )(*(pltpu.with_memory_space_constraint(v, pltpu.VMEM) for v in (p, q)))


def local(tokens, w_qk, w_in, w_out, particles, cotangent, clusters, owners):
    n_shard = lax.axis_size("shard")
    nzh = lax.axis_size("group") // NX
    nb = owners.shape[0]
    feat = particles.reshape(nb, BLOCK, -1)
    cot = cotangent.reshape(nb, BLOCK, -1)
    out, qk_grad = layer(
        owners.reshape(1, nb), clusters.reshape(nb, BLOCK), w_qk, tokens, w_in, w_out, feat, cot,
        nzh, n_shard // 4,
    )
    out, qk_grad = place(out, qk_grad)
    return (out.reshape(particles.shape), qk_grad)


def solution(mesh):
    placed = (
        P(("group", "shard"), None),
        P("shard", None),
        P(),
        P(),
        P(("group", "shard"), None),
        P(("group", "shard"), None),
        P(("group", "shard")),
        P(("group", "shard")),
    )
    return jax.shard_map(
        local,
        mesh=mesh,
        in_specs=placed,
        out_specs=(P(("group", "shard"), None), P("shard", None)),
        check_vma=False,
    )
```
